128 devices in a mesh: row: 8 (over z, x_hi), col: 16 (over y, x_lo, core).
Axes of the slice: x: 4 (x_hi: 2, x_lo: 2; x = x_hi * 2 + x_lo), y: 4, z: 4, core: 2. Of those that a mesh axis runs over, the one named last changes fastest.
Arguments:
- patches: bfloat16 [98304, 1536], P(('row', 'col')), may hold values from -6 to 6
- dest: int32 [98304], P(('row', 'col')), may hold values from -1 to 511, as said below
- background: bfloat16 [1536], replicated, may hold values from -6 to 6
- conv_weight: float32 [7, 7, 1536], replicated, may hold values from -0.875 to 0.875
- conv_bias: float32 [1536], replicated, may hold values from -3 to 3
- norm_gain: float32 [1536], replicated, may hold values from 0.1 to 1.9
- norm_bias: float32 [1536], replicated, may hold values from -3 to 3
- w_in: bfloat16 [6144, 1536], P('col'), may hold values from -0.15625 to 0.15625
- b_in: bfloat16 [6144], P('col'), may hold values from -3 to 3
- w_out: bfloat16 [6144, 1536], P('col'), may hold values from -0.078125 to 0.078125
- b_out: float32 [1536], replicated, may hold values from -3 to 3
- layer_scale: float32 [1536], replicated, may hold values from 0.3 to 1.5
Outputs:
- features: bfloat16 [256, 256, 1536], P('row', 'col')
The draws below stay inside these ranges and needn't reach their ends.
Inputs may be any that keep to these rules, and one draw needn't show every extreme that they name: `dest`: -1 marks an empty slot; no cell is named twice among all slots sent to one device; in every draw some device fills all 48 slots it sends to some device, and some device receives a patch for every one of its cells.
All inputs are finite; a program needn't handle non-finite values.
Results may differ from the reference program's by a relative error of at most 0.0046.
Values may be sent and summed in bfloat16 or wider, within the bound.
No kernel may reach another device: no remote copies, remote signals or barrier semaphores. Data moves between devices by JAX's collectives and lax.ppermute only.
A program may use at most 128 MiB of HBM per device.

```python
import math
import jax
import jax.numpy as jnp
from jax import lax

C = 1536
FF = 6144
TH = 32
TW = 16
NR = 256
NC = 256
CAP = 48
ROUTE_ROWS = 98304
N_ROW = 8
N_COL = 16


def draw_dest(key, part):
    cells = TH * TW
    slots = N_COL * CAP
    receivers = N_ROW * N_COL
    key_cells, key_slots, key_full, key_count = jax.random.split(key, 4)
    cell_order = jax.vmap(lambda k: jax.random.permutation(k, cells))(jax.random.split(key_cells, receivers))
    slot_order = jax.vmap(lambda k: jax.random.permutation(k, slots))(jax.random.split(key_slots, receivers))
    full_sender = jax.random.randint(key_full, (receivers,), 0, N_COL)
    sender_of_slot = jnp.arange(slots) // CAP
    scores = jnp.where(sender_of_slot[None, :] == full_sender[:, None], slot_order - 2 * slots, slot_order)
    order = jnp.argsort(scores, axis=1, stable=True)
    ranking = jnp.argsort(order, axis=1, stable=True)
    count = jnp.minimum(jax.random.randint(key_count, (receivers,), cells // 2, cells + cells // 4 + 1), cells)
    picked = jnp.take_along_axis(cell_order, jnp.minimum(ranking, cells - 1), axis=1)
    result = jnp.where(ranking < count[:, None], picked, -1)
    result = result.reshape(N_ROW, N_COL, N_COL, CAP).transpose(0, 2, 1, 3)
    return result.reshape(-1).astype(jnp.int32)


def level_of(rng, shape, pieces, low, high):
    def one(dim, blocks):
        steps = jax.random.uniform(jax.random.fold_in(jax.random.fold_in(rng, 6), dim), (blocks,), jnp.float32, low / len(pieces), high / len(pieces))
        return jnp.repeat(jnp.exp(steps), shape[dim] // blocks).reshape((-1,) + (1,) * (len(shape) - dim - 1))

    loudness = one(*pieces[0])
    for cut in pieces[1:]:
        loudness = loudness * one(*cut)
    return loudness


def noise(rng, shape, scale, reach, pieces=(), kind=jnp.bfloat16):
    values = jax.random.normal(rng, shape, jnp.float32) * scale
    if len(pieces) > 0:
        values = level_of(rng, shape, pieces, -0.22, 0.18) * values
    return jnp.clip(values, min=-reach, max=reach).astype(kind)


def setup_inputs(seed: int = 0) -> dict:
    arg_keys = jax.random.split(jax.random.key(seed), 13)
    return {
        "patches": noise(arg_keys[0], (ROUTE_ROWS, C), 1.0, 6.0, ((0, 128),)),
        "dest": draw_dest(jax.random.fold_in(arg_keys[12], 71), 0),
        "background": noise(arg_keys[2], (C,), 1.0, 6.0),
        "conv_weight": noise(arg_keys[3], (7, 7, C), 49 ** -0.5, 0.875, (), jnp.float32),
        "conv_bias": noise(arg_keys[4], (C,), 0.5, 3.0, (), jnp.float32),
        "norm_gain": jnp.clip(1.0 + 0.18 * jax.random.normal(arg_keys[5], (C,), jnp.float32), 0.1, 1.9),
        "norm_bias": noise(arg_keys[6], (C,), 0.5, 3.0, (), jnp.float32),
        "w_in": noise(arg_keys[7], (FF, C), C ** -0.5, 0.15625, ((0, 16),)),
        "b_in": noise(arg_keys[8], (FF,), 0.5, 3.0, ((0, 16),)),
        "w_out": noise(arg_keys[9], (FF, C), FF ** -0.5, 0.078125, ((0, 16),)),
        "b_out": noise(arg_keys[10], (C,), 0.5, 3.0, (), jnp.float32),
        "layer_scale": jnp.clip(jnp.exp(jax.random.uniform(arg_keys[11], (C,), jnp.float32, math.log(0.3), math.log(1.5))), 0.3, 1.5),
    }


def reference(patches, dest, background, conv_weight, conv_bias, norm_gain, norm_bias, w_in, b_in, w_out, b_out, layer_scale):
    slot = dest.reshape(N_ROW, N_COL, N_COL, CAP)
    row_ids = jnp.arange(N_ROW, dtype=jnp.int32)[:, None, None, None]
    recv_ids = jnp.arange(N_COL, dtype=jnp.int32)[None, None, :, None]
    grid_row = row_ids * TH + slot // TW
    grid_col = recv_ids * TW + slot % TW
    flat_index = jnp.where(slot >= 0, grid_row * NC + grid_col, NR * NC).reshape(-1).astype(jnp.int32)
    canvas = jnp.zeros((NR * NC, C), jnp.bfloat16).at[flat_index].set(patches, mode='drop')
    filled = jnp.zeros((NR * NC,), jnp.int32).at[flat_index].set(1, mode='drop')
    grid = jnp.where(filled[:, None] > 0, canvas, background[None, :]).reshape(NR, NC, C)
    padded = jnp.pad(grid.astype(jnp.float32), ((3, 3), (3, 3), (0, 0)))
    conv = jnp.zeros((NR, NC, C), jnp.float32) + conv_bias
    for across in range(7):
        for along in range(7):
            conv = conv + padded[across:across + NR, along:along + NC, :] * conv_weight[across, along]
    mean = lax.optimization_barrier(jnp.mean(conv, axis=-1, keepdims=True))
    centred = conv - mean
    var = lax.optimization_barrier(jnp.mean(centred * centred, axis=-1, keepdims=True))
    normed = (centred * lax.rsqrt(var + 1e-06) * norm_gain + norm_bias).astype(jnp.bfloat16)

    def pointwise(rows):
        pre = jnp.dot(rows, w_in.T, preferred_element_type=jnp.float32) + b_in.astype(jnp.float32)
        hidden = jax.nn.gelu(pre, approximate=False).astype(jnp.bfloat16)
        return jnp.dot(hidden, w_out, preferred_element_type=jnp.float32)
    mixed = lax.map(pointwise, normed)
    out = grid.astype(jnp.float32) + layer_scale * (mixed + b_out)
    return out.astype(jnp.bfloat16)
```

```python
import jax
import jax.numpy as jnp
from jax import lax
from jax.sharding import PartitionSpec as P

TH = 32
TW = 16
QR = 96
HALF = 2 * QR


def device_index(x, y, z, core):
    x, y, z = x % 4, y % 4, z % 4
    return (z * 2 + x // 2) * 16 + y * 4 + (x % 2) * 2 + core


def routes(move):
    return [
        (device_index(x, y, z, core), device_index(*move(x, y, z, core)))
        for x in range(4)
        for y in range(4)
        for z in range(4)
        for core in range(2)
    ]


def send(value, move):
    return lax.ppermute(value, ("row", "col"), routes(move))


def to_partner(x, y, z, core):
    return x, y, z, 1 - core


def along_y(x, y, z, core):
    return x, y + 1 - 2 * core, z, core


def along_z(x, y, z, core):
    return x, y, z + 1 - 2 * core, core


def along_x(x, y, z, core):
    return x + 1 - 2 * core, y, z, core


def back_x(x, y, z, core):
    return x - 1 + 2 * core, y, z, core


def extended(cells, sides, width):
    for axis, dim in sides:
        count = lax.axis_size(axis)
        ends = count - 1
        head = lax.slice_in_dim(cells, 0, width, axis=dim)
        tail = lax.slice_in_dim(cells, cells.shape[dim] - width, cells.shape[dim], axis=dim)
        cells = jnp.concatenate(
            [
                lax.ppermute(tail, axis, [(i, (i + 1) % count) for i in range(ends)]),
                cells,
                lax.ppermute(head, axis, [((i + 1) % count, i) for i in range(ends)]),
            ],
            axis=dim,
        )
    return cells


def split_rows(pieces):
    ins, outs = [], []
    for piece in pieces:
        for k in range(piece.shape[0] // HALF):
            ins.append(piece[k * HALF : k * HALF + QR])
            outs.append(piece[k * HALF + QR : (k + 1) * HALF])
    return jnp.concatenate(ins, axis=0), jnp.concatenate(outs, axis=0)


def mlp(rows, groups):
    total = None
    for pieces, bias in groups:
        w_in, w_out = split_rows(pieces)
        pre = lax.dot_general(
            rows, w_in, (((1,), (1,)), ((), ())), preferred_element_type=jnp.float32
        )
        hidden = jax.nn.gelu(pre + bias.astype(jnp.float32), approximate=False).astype(jnp.bfloat16)
        part = jnp.dot(hidden, w_out, preferred_element_type=jnp.float32)
        total = part if total is None else total + part
    return total


def local(
    patches,
    dest,
    background,
    conv_weight,
    conv_bias,
    norm_gain,
    norm_bias,
    w_in,
    b_in,
    w_out,
    b_out,
    layer_scale,
):
    cells = TH * TW
    channels = patches.shape[1]
    row, col = lax.axis_index("row"), lax.axis_index("col")
    my_y, my_lo, my_core, my_h = col // 4, (col // 2) % 2, col % 2, (row // 2) % 2

    lane = lax.broadcasted_iota(jnp.int32, (768, 128), 1)
    high, low = (dest >> 4)[:, None], (dest & 15)[:, None]
    spread = jnp.pad(b_in.reshape(48, 8), ((0, 0), (8, 112)))
    extra = jnp.where(
        lane == 0,
        high.astype(jnp.bfloat16),
        jnp.where(lane == 1, low.astype(jnp.bfloat16), jnp.tile(spread, (16, 1))),
    )
    moved = lax.all_to_all(
        jnp.concatenate([patches, extra], axis=1), "col", split_axis=0, concat_axis=0, tiled=True
    )

    own = jnp.concatenate(
        [part for q in range(4) for part in (w_in[q * QR : (q + 1) * QR], w_out[q * QR : (q + 1) * QR])],
        axis=0,
    )
    partner = send(own, to_partner)
    first = jnp.concatenate(
        [lax.dynamic_slice_in_dim(v, my_h * 2 * HALF, 2 * HALF, axis=0) for v in (own, partner)], axis=0
    )
    near = send(first, along_y)
    near_p = send(near, to_partner)
    near_z = send(near, along_z)
    far = send(near[: 2 * HALF], along_y)
    far_z = send(far, along_z)
    near_zp = send(near_z, to_partner)
    far_p = send(far, to_partner)
    far_zp = send(far_z, to_partner)

    bias = moved[:, channels + 8 : channels + 16].reshape(4, 2, 2, 2, HALF)
    bias = lax.dynamic_index_in_dim(bias, my_lo, axis=1, keepdims=False)
    bias = jnp.where(my_core == 1, bias[:, ::-1], bias)
    turned = jnp.where(my_h == 1, bias[:, :, ::-1], bias)
    ahead = 2 * my_core - 1

    def at(array, step):
        return lax.dynamic_index_in_dim(array, (my_y + step + 4) % 4, axis=0, keepdims=False)

    b_one, b_two, b_far = at(turned, ahead), at(turned, -ahead), at(turned, 2)
    b0 = at(bias, 0).reshape(-1)
    b1 = jnp.concatenate([b_one[0, 0], b_one[1, 0], b_two[1, 0], b_two[0, 0]])
    b2 = jnp.concatenate([b_one[0, 1], b_one[1, 1], b_two[1, 1], b_two[0, 1]])
    b3 = jnp.concatenate([b_far[0, 0], b_far[1, 0], b_far[0, 1], b_far[1, 1]])
    early = [((own, partner), b0), ((near, near_p), b1)]
    late = [((near_z, near_zp), b2), ((far, far_p, far_z, far_zp), b3)]

    where = (moved[:, channels].astype(jnp.int32) << 4) + moved[:, channels + 1].astype(jnp.int32)
    onehot = where[None, :] == jnp.arange(cells, dtype=jnp.int32)[:, None]
    placed = jnp.dot(
        onehot.astype(jnp.bfloat16), moved[:, :channels], preferred_element_type=jnp.float32
    )
    present = jnp.any(onehot, axis=1)
    grid = jnp.where(present[:, None], placed, background.astype(jnp.float32)[None, :]).astype(
        jnp.bfloat16
    )
    padded = extended(grid.reshape(TH, TW, channels), (("row", 0), ("col", 1)), 3)
    conv = jnp.zeros((TH, TW, channels), jnp.float32) + conv_bias
    for across in range(7):
        for along in range(7):
            conv = (
                conv
                + padded[across : across + TH, along : along + TW, :].astype(jnp.float32)
                * conv_weight[across, along]
            )
    mean = jnp.mean(conv, axis=-1, keepdims=True)
    centred = conv - mean
    var = jnp.mean(centred * centred, axis=-1, keepdims=True)
    normed = (centred * lax.rsqrt(var + 1e-06) * norm_gain + norm_bias).astype(jnp.bfloat16)
    flat = normed.reshape(cells, channels)

    other = send(flat, along_x)
    mine = mlp(flat, early + late)
    theirs = mlp(other, early + late).astype(jnp.bfloat16)
    returned = send(theirs, back_x)
    mixed = mine + returned.astype(jnp.float32)
    result = grid.astype(jnp.float32) + layer_scale * (mixed + b_out)
    return result.astype(jnp.bfloat16).reshape(TH, TW, channels)


def solution(mesh):
    placed = (
        P(("row", "col"), None),
        P(("row", "col")),
        P(),
        P(),
        P(),
        P(),
        P(),
        P("col", None),
        P("col"),
        P("col", None),
        P(),
        P(),
    )
    return jax.shard_map(
        local, mesh=mesh, in_specs=placed, out_specs=P("row", "col", None), check_vma=False
    )
```

```python
import functools

import jax
import jax.numpy as jnp
from jax import lax
from jax.experimental import pallas as pl
from jax.experimental.pallas import tpu as pltpu
from jax.sharding import PartitionSpec as P

TH = 32
TW = 16
SHARD = 384
HALF = SHARD // 2
LANES = 128
EXTRA = 128
BAND = 8
ROWS = 256
UNITS = 256

VMEM = pltpu.VMEM


def device_index(x, y, z, core):
    x, y, z = x % 4, y % 4, z % 4
    return (z * 2 + x // 2) * 16 + y * 4 + (x % 2) * 2 + core


def routes(move):
    return [
        (device_index(x, y, z, core), device_index(*move(x, y, z, core)))
        for x in range(4)
        for y in range(4)
        for z in range(4)
        for core in range(2)
    ]


def send(value, move):
    return lax.ppermute(value, ("row", "col"), routes(move))


def to_partner(x, y, z, core):
    return x, y, z, 1 - core


def along_y(x, y, z, core):
    return x, y + 1 - 2 * core, z, core


def along_z(x, y, z, core):
    return x, y, z + 1 - 2 * core, core


def along_x(x, y, z, core):
    return x + 1 - 2 * core, y, z, core


def back_x(x, y, z, core):
    return x - 1 + 2 * core, y, z, core


def halo(cells, axis, dim, width):
    count = lax.axis_size(axis)
    ends = count - 1
    head = lax.slice_in_dim(cells, 0, width, axis=dim)
    tail = lax.slice_in_dim(cells, cells.shape[dim] - width, cells.shape[dim], axis=dim)
    return (
        lax.ppermute(tail, axis, [(i, i + 1) for i in range(ends)]),
        lax.ppermute(head, axis, [(i + 1, i) for i in range(ends)]),
    )


def whole(space=VMEM):
    return pl.BlockSpec(memory_space=space)


def join_kernel(left_ref, right_ref, out_ref):
    split = left_ref.shape[1]
    out_ref[:, :split] = left_ref[...]
    out_ref[:, split:] = right_ref[...]


def join(left, right):
    rows, a = left.shape
    b = right.shape[1]
    block = 128
    return pl.pallas_call(
        join_kernel,
        out_shape=jax.ShapeDtypeStruct((rows, a + b), left.dtype),
        grid=(rows // block,),
        in_specs=[pl.BlockSpec((block, a), lambda i: (i, 0)), pl.BlockSpec((block, b), lambda i: (i, 0))],
        out_specs=pl.BlockSpec((block, a + b), lambda i: (i, 0)),
        cost_estimate=pl.CostEstimate(flops=0, bytes_accessed=4 * rows * (a + b), transcendentals=0),
        name="join",
    )(left, right)


def stack_kernel(half_ref, *refs):
    sources, out_ref, sems = refs[:4], refs[4], refs[5]
    start = pl.multiple_of(half_ref[0] * HALF, HALF)
    copies = [
        pltpu.make_async_copy(source.at[pl.ds(start, HALF)], out_ref.at[pl.ds(k * HALF, HALF)], sems.at[k])
        for k, source in enumerate(sources)
    ]
    for copy in copies:
        copy.start()
    for copy in copies:
        copy.wait()


def stack(half, *sources):
    channels = sources[0].shape[1]
    return pl.pallas_call(
        stack_kernel,
        out_shape=jax.ShapeDtypeStruct((4 * HALF, channels), jnp.bfloat16),
        in_specs=[whole(pltpu.SMEM)] + [whole(pl.ANY)] * 4,
        out_specs=whole(),
        scratch_shapes=[pltpu.SemaphoreType.DMA((4,))],
        cost_estimate=pl.CostEstimate(flops=0, bytes_accessed=16 * HALF * channels, transcendentals=0),
        name="stack",
    )(half, *sources)


def conv_norm_kernel(
    grid_ref, top_ref, bottom_ref, left_ref, right_ref, weight_ref, bias_ref, gain_ref, shift_ref,
    out_ref, stage, conv,
):
    channels = grid_ref.shape[2]
    tiles = channels // LANES

    def tile(t, carry):
        at = pl.ds(pl.multiple_of(t * LANES, LANES), LANES)
        stage[3 : 3 + TH, 8:24, :] = grid_ref[:, :, at].astype(jnp.float32)
        stage[0:3, 8:24, :] = top_ref[:, :, at].astype(jnp.float32)
        stage[3 + TH : 6 + TH, 8:24, :] = bottom_ref[:, :, at].astype(jnp.float32)
        stage[:, 5:8, :] = left_ref[:, :, at].astype(jnp.float32)
        stage[:, 24:27, :] = right_ref[:, :, at].astype(jnp.float32)
        base = jnp.broadcast_to(bias_ref[0:1, at], (TW, LANES))

        def band(b, carry):
            acc = [base] * BAND
            for along in range(7):
                taps = [
                    jnp.broadcast_to(weight_ref[across * 7 + along : across * 7 + along + 1, at], (TW, LANES))
                    for across in range(7)
                ]
                for r in range(BAND + 6):
                    value = stage[b * BAND + r, 5 + along : 5 + along + TW, :]
                    for across in range(7):
                        o = r - across
                        if 0 <= o < BAND:
                            acc[o] = acc[o] + value * taps[across]
            for o in range(BAND):
                conv[t, pl.ds(pl.multiple_of((b * BAND + o) * TW, TW), TW), :] = acc[o]
            return carry

        return lax.fori_loop(0, TH // BAND, band, carry)

    lax.fori_loop(0, tiles, tile, 0)

    def norm(b, carry):
        rows = pl.ds(pl.multiple_of(b * 16, 16), 16)
        values = [conv[t, rows, :] for t in range(tiles)]
        mean = jnp.sum(sum(values), axis=-1, keepdims=True) * (1.0 / channels)
        centred = [v - mean for v in values]
        var = jnp.sum(sum(v * v for v in centred), axis=-1, keepdims=True) * (1.0 / channels)
        inverse = lax.rsqrt(var + 1e-06)
        for t in range(tiles):
            at = slice(t * LANES, (t + 1) * LANES)
            out_ref[rows, at] = (centred[t] * inverse * gain_ref[0:1, at] + shift_ref[0:1, at]).astype(
                jnp.bfloat16
            )
        return carry

    lax.fori_loop(0, TH * TW // 16, norm, 0)


def conv_norm(grid, top, bottom, left, right, weight, bias, gain, shift):
    channels = grid.shape[2]
    return pl.pallas_call(
        conv_norm_kernel,
        out_shape=jax.ShapeDtypeStruct((TH * TW, channels), jnp.bfloat16),
        in_specs=[whole()] * 9,
        out_specs=whole(),
        scratch_shapes=[
            VMEM((TH + 6, 32, LANES), jnp.float32),
            VMEM((channels // LANES, TH * TW, LANES), jnp.float32),
        ],
        cost_estimate=pl.CostEstimate(
            flops=100 * TH * TW * channels, bytes_accessed=8 * TH * TW * channels, transcendentals=0
        ),
        name="conv_norm",
    )(grid, top, bottom, left, right, weight.reshape(49, channels), bias[None], gain[None], shift[None])


PHI = (
    0.7978849411010742, 0.03633308410644531, -3.259496588725597e-05, -5.5306198191829026e-05,
    3.964745246776147e-06, -1.3226342332472996e-07, 1.7561730958348676e-09,
)


def gelu(pre):
    x = jnp.clip(pre, -5.3, 5.3)
    s = x * x
    p = PHI[-1]
    for c in PHI[-2::-1]:
        p = p * s + c
    half = 0.5 * pre
    return half + half * jnp.tanh(x * p)


def mlp_kernel(plan, count, adds, *refs):
    x_ref, bias_ref = refs[:2]
    pieces = refs[2 : 2 + count]
    acc_ref = refs[2 + count] if adds else None
    out_ref, w_in, w_out, hid, sems = refs[2 + count + adds :]
    blocks = w_in.shape[0] // UNITS
    bands = x_ref.shape[0] // ROWS
    ins, outs, at = [], [], 0
    for k, (a, row_a, b, row_b, size) in enumerate(plan):
        ins.append(pltpu.make_async_copy(pieces[a].at[pl.ds(row_a, size)], w_in.at[pl.ds(at, size)], sems.at[k, 0]))
        outs.append(pltpu.make_async_copy(pieces[b].at[pl.ds(row_b, size)], w_out.at[pl.ds(at, size)], sems.at[k, 1]))
        at += size
    for copy in ins + outs:
        copy.start()
    early = next(k for k in range(len(plan) + 1) if sum(p[4] for p in plan[:k]) >= 3 * UNITS)

    def first(r, h):
        return lax.dot_general(
            x_ref[r * ROWS : (r + 1) * ROWS, :],
            w_in[h * UNITS : (h + 1) * UNITS, :],
            (((1,), (1,)), ((), ())),
            preferred_element_type=jnp.float32,
        )

    def middle(r, h, pre):
        at = slice(h * UNITS, (h + 1) * UNITS)
        hid[r * ROWS : (r + 1) * ROWS, at] = gelu(pre + bias_ref[0:1, at]).astype(jnp.bfloat16)

    def second(r, n):
        rows, at = slice(r * ROWS, (r + 1) * ROWS), slice(n * UNITS, (n + 1) * UNITS)
        total = jnp.dot(hid[rows, :], w_out[:, at], preferred_element_type=jnp.float32)
        if adds:
            total = total + acc_ref[rows, at]
        out_ref[rows, at] = total.astype(out_ref.dtype)

    tasks = [(r, h) for r in range(bands) for h in range(blocks)]
    done = [(r, n) for r in range(bands) for n in range(w_out.shape[1] // UNITS)]
    for copy in ins[:early]:
        copy.wait()
    waiting, sent = None, 0
    for k, (r, h) in enumerate(tasks):
        if k == 3:
            for copy in ins[early:] + outs:
                copy.wait()
        pre = first(r, h)
        if waiting is not None:
            middle(*waiting)
        waiting = (r, h, pre)
        if r > 0 and h > 0:
            second(*done[sent])
            sent += 1
    middle(*waiting)
    for item in done[sent:]:
        second(*item)


def mlp(x, bias, pieces, plan, acc=None, out_dtype=jnp.float32):
    m, channels = x.shape
    hidden = sum(p[4] for p in plan)
    adds = acc is not None
    return pl.pallas_call(
        functools.partial(mlp_kernel, plan, len(pieces), int(adds)),
        out_shape=jax.ShapeDtypeStruct((m, channels), out_dtype),
        in_specs=[whole()] * 2 + [whole(pl.ANY)] * len(pieces) + [whole()] * adds,
        out_specs=whole(),
        scratch_shapes=[
            VMEM((hidden, channels), jnp.bfloat16),
            VMEM((hidden, channels), jnp.bfloat16),
            VMEM((m, hidden), jnp.bfloat16),
            pltpu.SemaphoreType.DMA((len(plan), 2)),
        ],
        cost_estimate=pl.CostEstimate(
            flops=4 * m * hidden * channels, bytes_accessed=4 * hidden * channels, transcendentals=m * hidden
        ),
        name="mlp",
    )(x, bias.reshape(1, hidden), *pieces, *([acc] if adds else []))


def local(
    patches,
    dest,
    background,
    conv_weight,
    conv_bias,
    norm_gain,
    norm_bias,
    w_in,
    b_in,
    w_out,
    b_out,
    layer_scale,
):
    cells = TH * TW
    channels = patches.shape[1]
    row, col = lax.axis_index("row"), lax.axis_index("col")
    my_y, my_lo, my_core, my_h = col // 4, (col // 2) % 2, col % 2, (row // 2) % 2

    lane = lax.broadcasted_iota(jnp.int32, (768, 128), 1)
    high, low = (dest >> 4)[:, None], (dest & 15)[:, None]
    spread = jnp.pad(b_in.reshape(48, 8), ((0, 0), (8, 112)))
    extra = jnp.where(
        lane == 0,
        high.astype(jnp.bfloat16),
        jnp.where(lane == 1, low.astype(jnp.bfloat16), jnp.tile(spread, (16, 1))),
    )
    moved = lax.all_to_all(join(patches, extra), "col", split_axis=0, concat_axis=0, tiled=True)

    w_in_p, w_out_p = send(w_in, to_partner), send(w_out, to_partner)
    near = send(stack(my_h.astype(jnp.int32).reshape(1), w_in, w_out, w_in_p, w_out_p), along_y)
    near_p = send(near, to_partner)
    near_z = send(near, along_z)
    far = send(near[: 2 * HALF], along_y)
    far_z = send(far, along_z)
    near_zp = send(near_z, to_partner)
    far_p = send(far, to_partner)
    far_zp = send(far_z, to_partner)

    bias = moved[:, channels + 8 : channels + 16].reshape(4, 2, 2, 2, HALF)
    bias = lax.dynamic_index_in_dim(bias, my_lo, axis=1, keepdims=False)
    bias = jnp.where(my_core == 1, bias[:, ::-1], bias)
    turned = jnp.where(my_h == 1, bias[:, :, ::-1], bias)
    ahead = 2 * my_core - 1

    def at(array, step):
        return lax.dynamic_index_in_dim(array, (my_y + step + 4) % 4, axis=0, keepdims=False)

    b_one, b_two, b_far = at(turned, ahead), at(turned, -ahead), at(turned, 2)
    b0 = at(bias, 0).reshape(-1)
    b1 = jnp.concatenate([b_one[0, 0], b_one[1, 0], b_two[1, 0], b_two[0, 0]])
    b2 = jnp.concatenate([b_one[0, 1], b_one[1, 1], b_two[1, 1], b_two[0, 1]])
    b3 = jnp.concatenate([b_far[0, 0], b_far[1, 0], b_far[0, 1], b_far[1, 1]])
    early = (w_in, w_out, w_in_p, w_out_p, near, near_p)
    early_plan = ((0, 0, 1, 0, SHARD), (2, 0, 3, 0, SHARD)) + tuple(
        (a, row, a, row + HALF, HALF) for a in (4, 5) for row in (0, 2 * HALF)
    )
    early_bias = jnp.concatenate([b0, b1]).astype(jnp.float32)
    late = (near_z, near_zp, far, far_p, far_z, far_zp)
    late_plan = tuple((a, row, a, row + HALF, HALF) for a in (0, 1) for row in (0, 2 * HALF)) + tuple(
        (a, 0, a, HALF, HALF) for a in (2, 3, 4, 5)
    )
    late_bias = jnp.concatenate([b2, b3]).astype(jnp.float32)

    where = (moved[:, channels].astype(jnp.int32) << 4) + moved[:, channels + 1].astype(jnp.int32)
    onehot = where[None, :] == jnp.arange(cells, dtype=jnp.int32)[:, None]
    placed = jnp.dot(
        onehot.astype(jnp.bfloat16), moved[:, :channels], preferred_element_type=jnp.float32
    )
    present = jnp.any(onehot, axis=1)
    grid = jnp.where(present[:, None], placed, background.astype(jnp.float32)[None, :]).astype(
        jnp.bfloat16
    )
    block = grid.reshape(TH, TW, channels)
    top, bottom = halo(block, "row", 0, 3)
    tall = [
        jnp.concatenate([part[:, cut] for part in (top, block, bottom)], axis=0)
        for cut in (slice(TW - 3, TW), slice(0, 3))
    ]
    ends = lax.axis_size("col") - 1
    left = lax.ppermute(tall[0], "col", [(i, i + 1) for i in range(ends)])
    right = lax.ppermute(tall[1], "col", [(i + 1, i) for i in range(ends)])
    flat = conv_norm(block, top, bottom, left, right, conv_weight, conv_bias, norm_gain, norm_bias)

    other = send(flat, along_x)
    mine = mlp(flat, early_bias, early, early_plan)
    theirs = mlp(other, early_bias, early, early_plan)
    theirs = mlp(other, late_bias, late, late_plan, acc=theirs, out_dtype=jnp.bfloat16)
    returned = send(theirs, back_x)
    mine = mlp(flat, late_bias, late, late_plan, acc=mine)
    mixed = mine + returned.astype(jnp.float32)
    result = grid.astype(jnp.float32) + layer_scale * (mixed + b_out)
    return result.astype(jnp.bfloat16).reshape(TH, TW, channels)


def solution(mesh):
    placed = (
        P(("row", "col"), None),
        P(("row", "col")),
        P(),
        P(),
        P(),
        P(),
        P(),
        P("col", None),
        P("col"),
        P("col", None),
        P(),
        P(),
    )
    return jax.shard_map(
        local, mesh=mesh, in_specs=placed, out_specs=P("row", "col", None), check_vma=False
    )
```

```python
import functools

import jax
import jax.numpy as jnp
from jax import lax
from jax.experimental import pallas as pl
from jax.experimental.pallas import tpu as pltpu
from jax.sharding import PartitionSpec as P


TH = 32
TW = 16
SHARD = 384
HALF = SHARD // 2
LANES = 128
BAND = 8
ROWS = 256
UNITS = 256

VMEM = pltpu.VMEM


def device_index(x, y, z, core):
    x, y, z = x % 4, y % 4, z % 4
    return (z * 2 + x // 2) * 16 + y * 4 + (x % 2) * 2 + core


def routes(move):
    return [
        (device_index(x, y, z, core), device_index(*move(x, y, z, core)))
        for x in range(4)
        for y in range(4)
        for z in range(4)
        for core in range(2)
    ]


def send(value, move):
    return lax.ppermute(value, ("row", "col"), routes(move))


def to_partner(x, y, z, core):
    return x, y, z, 1 - core


def along_y(x, y, z, core):
    return x, y + 1 - 2 * core, z, core


def along_z(x, y, z, core):
    return x, y, z + 1 - 2 * core, core


def along_x(x, y, z, core):
    return x + 1 - 2 * core, y, z, core


def back_x(x, y, z, core):
    return x - 1 + 2 * core, y, z, core


def halo(cells, axis, dim, width):
    count = lax.axis_size(axis)
    ends = count - 1
    head = lax.slice_in_dim(cells, 0, width, axis=dim)
    tail = lax.slice_in_dim(cells, cells.shape[dim] - width, cells.shape[dim], axis=dim)
    return (
        lax.ppermute(tail, axis, [(i, i + 1) for i in range(ends)]),
        lax.ppermute(head, axis, [(i + 1, i) for i in range(ends)]),
    )


def whole(space=VMEM):
    return pl.BlockSpec(memory_space=space)


def join_kernel(left_ref, right_ref, out_ref):
    split = left_ref.shape[1]
    out_ref[:, :split] = left_ref[...]
    out_ref[:, split:] = right_ref[...]


def join(left, right):
    rows, a = left.shape
    b = right.shape[1]
    block = 128
    return pl.pallas_call(
        join_kernel,
        out_shape=jax.ShapeDtypeStruct((rows, a + b), left.dtype),
        grid=(rows // block,),
        in_specs=[pl.BlockSpec((block, a), lambda i: (i, 0)), pl.BlockSpec((block, b), lambda i: (i, 0))],
        out_specs=pl.BlockSpec((block, a + b), lambda i: (i, 0)),
        cost_estimate=pl.CostEstimate(flops=0, bytes_accessed=4 * rows * (a + b), transcendentals=0),
        name="join",
    )(left, right)


def stack_kernel(half_ref, *refs):
    *sources, out_ref, sems = refs
    start = pl.multiple_of(half_ref[0] * HALF, HALF)
    copies = [
        pltpu.make_async_copy(source.at[pl.ds(start, HALF)], out_ref.at[pl.ds(k * HALF, HALF)], sems.at[k])
        for k, source in enumerate(sources)
    ]
    for copy in copies:
        copy.start()
    for copy in copies:
        copy.wait()


def stack(half, *sources):
    channels = sources[0].shape[1]
    return pl.pallas_call(
        stack_kernel,
        out_shape=jax.ShapeDtypeStruct((len(sources) * HALF, channels), jnp.bfloat16),
        in_specs=[whole(pltpu.SMEM)] + [whole(pl.ANY)] * len(sources),
        out_specs=whole(),
        scratch_shapes=[pltpu.SemaphoreType.DMA((len(sources),))],
        cost_estimate=pl.CostEstimate(flops=0, bytes_accessed=4 * len(sources) * HALF * channels, transcendentals=0),
        name="stack",
    )(half, *sources)


def conv_kernel(first, count, ends, *refs):
    grid_ref, top_ref, bottom_ref, left_ref, right_ref, weight_ref, bias_ref = refs[:7]
    if ends:
        gain_ref, shift_ref, before, out_ref, stage, conv = refs[7:]
    else:
        conv, stage = refs[7:]

    def tile(t, carry):
        at = pl.ds(pl.multiple_of((first + t) * LANES, LANES), LANES)
        stage[3 : 3 + TH, 8:24, :] = grid_ref[:, :, at].astype(jnp.float32)
        stage[0:3, 8:24, :] = top_ref[:, :, at].astype(jnp.float32)
        stage[3 + TH : 6 + TH, 8:24, :] = bottom_ref[:, :, at].astype(jnp.float32)
        stage[:, 5:8, :] = left_ref[:, :, at].astype(jnp.float32)
        stage[:, 24:27, :] = right_ref[:, :, at].astype(jnp.float32)
        base = jnp.broadcast_to(bias_ref[0:1, at], (TW, LANES))

        def band(b, carry):
            acc = [base] * BAND
            for along in range(7):
                taps = [
                    jnp.broadcast_to(weight_ref[across * 7 + along : across * 7 + along + 1, at], (TW, LANES))
                    for across in range(7)
                ]
                for r in range(BAND + 6):
                    value = stage[b * BAND + r, 5 + along : 5 + along + TW, :]
                    for across in range(7):
                        o = r - across
                        if 0 <= o < BAND:
                            acc[o] = acc[o] + value * taps[across]
            for o in range(BAND):
                conv[t, pl.ds(pl.multiple_of((b * BAND + o) * TW, TW), TW), :] = acc[o]
            return carry

        return lax.fori_loop(0, TH // BAND, band, carry)

    lax.fori_loop(0, count, tile, 0)
    if not ends:
        return
    tiles = first + count
    channels = tiles * LANES

    def norm(b, carry):
        rows = pl.ds(pl.multiple_of(b * 16, 16), 16)
        values = [before[t, rows, :] for t in range(first)] + [conv[t, rows, :] for t in range(count)]
        mean = jnp.sum(sum(values), axis=-1, keepdims=True) * (1.0 / channels)
        centred = [v - mean for v in values]
        var = jnp.sum(sum(v * v for v in centred), axis=-1, keepdims=True) * (1.0 / channels)
        inverse = lax.rsqrt(var + 1e-06)
        for t in range(tiles):
            at = slice(t * LANES, (t + 1) * LANES)
            out_ref[rows, at] = (centred[t] * inverse * gain_ref[0:1, at] + shift_ref[0:1, at]).astype(
                jnp.bfloat16
            )
        return carry

    lax.fori_loop(0, TH * TW // 16, norm, 0)


def conv_call(first, count, inputs, ends=None):
    tiles = VMEM((count, TH * TW, LANES), jnp.float32)
    stage = VMEM((TH + 6, 32, LANES), jnp.float32)
    if ends is None:
        out, scratch, more = jax.ShapeDtypeStruct(tiles.shape, jnp.float32), [stage], ()
    else:
        out = jax.ShapeDtypeStruct((TH * TW, (first + count) * LANES), jnp.bfloat16)
        scratch, more = [stage, tiles], ends
    return pl.pallas_call(
        functools.partial(conv_kernel, first, count, ends is not None),
        out_shape=out,
        in_specs=[whole()] * (7 + len(more)),
        out_specs=whole(),
        scratch_shapes=scratch,
        cost_estimate=pl.CostEstimate(
            flops=100 * TH * TW * count * LANES, bytes_accessed=8 * TH * TW * count * LANES, transcendentals=0
        ),
        name="conv",
    )(*inputs, *more)


PHI = (
    0.7978849411010742, 0.03633308410644531, -3.259496588725597e-05, -5.5306198191829026e-05,
    3.964745246776147e-06, -1.3226342332472996e-07, 1.7561730958348676e-09,
)


def gelu(pre):
    x = jnp.clip(pre, -5.3, 5.3)
    s = x * x
    p = PHI[-1]
    for c in PHI[-2::-1]:
        p = p * s + c
    half = 0.5 * pre
    return half + half * jnp.tanh(x * p)


def mlp_kernel(plan, count, adds, *refs):
    x_ref, bias_ref = refs[:2]
    pieces = refs[2 : 2 + count]
    acc_ref = refs[2 + count] if adds else None
    out_ref, w_in, w_out, hid, sems = refs[2 + count + adds :]
    blocks = w_in.shape[0] // UNITS
    bands = x_ref.shape[0] // ROWS
    ins, outs, at = [], [], 0
    for k, (a, row_a, b, row_b, size) in enumerate(plan):
        ins.append(pltpu.make_async_copy(pieces[a].at[pl.ds(row_a, size)], w_in.at[pl.ds(at, size)], sems.at[k, 0]))
        outs.append(pltpu.make_async_copy(pieces[b].at[pl.ds(row_b, size)], w_out.at[pl.ds(at, size)], sems.at[k, 1]))
        at += size
    for copy in ins + outs:
        copy.start()
    early = next(k for k in range(len(plan) + 1) if sum(p[4] for p in plan[:k]) >= 3 * UNITS)

    def first(r, h):
        return lax.dot_general(
            x_ref[r * ROWS : (r + 1) * ROWS, :],
            w_in[h * UNITS : (h + 1) * UNITS, :],
            (((1,), (1,)), ((), ())),
            preferred_element_type=jnp.float32,
        )

    def middle(r, h, pre):
        at = slice(h * UNITS, (h + 1) * UNITS)
        hid[r * ROWS : (r + 1) * ROWS, at] = gelu(pre + bias_ref[0:1, at]).astype(jnp.bfloat16)

    def second(r, n):
        rows, at = slice(r * ROWS, (r + 1) * ROWS), slice(n * UNITS, (n + 1) * UNITS)
        total = jnp.dot(hid[rows, :], w_out[:, at], preferred_element_type=jnp.float32)
        if adds:
            total = total + acc_ref[rows, at]
        out_ref[rows, at] = total.astype(out_ref.dtype)

    tasks = [(r, h) for r in range(bands) for h in range(blocks)]
    done = [(r, n) for r in range(bands) for n in range(w_out.shape[1] // UNITS)]
    for copy in ins[:early]:
        copy.wait()
    waiting, sent = None, 0
    for k, (r, h) in enumerate(tasks):
        if k == 3:
            for copy in ins[early:] + outs:
                copy.wait()
        pre = first(r, h)
        if waiting is not None:
            middle(*waiting)
        waiting = (r, h, pre)
        if r > 0 and h > 0:
            second(*done[sent])
            sent += 1
    middle(*waiting)
    for item in done[sent:]:
        second(*item)


def mlp(x, bias, pieces, plan, acc=None, out_dtype=jnp.float32):
    m, channels = x.shape
    hidden = sum(p[4] for p in plan)
    adds = acc is not None
    return pl.pallas_call(
        functools.partial(mlp_kernel, plan, len(pieces), int(adds)),
        out_shape=jax.ShapeDtypeStruct((m, channels), out_dtype),
        in_specs=[whole()] * 2 + [whole(pl.ANY)] * len(pieces) + [whole()] * adds,
        out_specs=whole(),
        scratch_shapes=[
            VMEM((hidden, channels), jnp.bfloat16),
            VMEM((hidden, channels), jnp.bfloat16),
            VMEM((m, hidden), jnp.bfloat16),
            pltpu.SemaphoreType.DMA((len(plan), 2)),
        ],
        cost_estimate=pl.CostEstimate(
            flops=4 * m * hidden * channels, bytes_accessed=4 * hidden * channels, transcendentals=m * hidden
        ),
        name="mlp",
    )(x, bias.reshape(1, hidden), *pieces, *([acc] if adds else []))


def local(
    patches,
    dest,
    background,
    conv_weight,
    conv_bias,
    norm_gain,
    norm_bias,
    w_in,
    b_in,
    w_out,
    b_out,
    layer_scale,
):
    cells = TH * TW
    channels = patches.shape[1]
    row, col = lax.axis_index("row"), lax.axis_index("col")
    my_y, my_lo, my_core, my_h = col // 4, (col // 2) % 2, col % 2, (row // 2) % 2

    lane = lax.broadcasted_iota(jnp.int32, (768, 128), 1)
    high, low = (dest >> 4)[:, None], (dest & 15)[:, None]
    spread = jnp.pad(b_in.reshape(48, 8), ((0, 0), (8, 112)))
    extra = jnp.where(
        lane == 0,
        high.astype(jnp.bfloat16),
        jnp.where(lane == 1, low.astype(jnp.bfloat16), jnp.tile(spread, (16, 1))),
    )
    moved = lax.all_to_all(join(patches, extra), "col", split_axis=0, concat_axis=0, tiled=True)

    w_in_p, w_out_p = send(w_in, to_partner), send(w_out, to_partner)
    half = my_h.astype(jnp.int32).reshape(1)
    near_a = send(stack(half, w_in, w_out), along_y)
    near_b = send(stack(half, w_in_p, w_out_p), along_y)
    near_a_z = send(near_a, along_z)
    far = send(near_a, along_y)
    near_a_p = send(near_a, to_partner)
    near_b_z = send(near_b, along_z)
    near_b_p = send(near_b, to_partner)
    far_z = send(far, along_z)
    far_p = send(far, to_partner)
    near_a_zp = send(near_a_z, to_partner)
    near_b_zp = send(near_b_z, to_partner)
    far_zp = send(far_z, to_partner)

    bias = moved[:, channels + 8 : channels + 16].reshape(4, 2, 2, 2, HALF)
    bias = lax.dynamic_index_in_dim(bias, my_lo, axis=1, keepdims=False)
    bias = jnp.where(my_core == 1, bias[:, ::-1], bias)
    turned = jnp.where(my_h == 1, bias[:, :, ::-1], bias)
    ahead = 2 * my_core - 1

    def at(array, step):
        return lax.dynamic_index_in_dim(array, (my_y + step + 4) % 4, axis=0, keepdims=False)

    b_one, b_two, b_far = at(turned, ahead), at(turned, -ahead), at(turned, 2)
    b0 = at(bias, 0).reshape(-1)
    b1 = jnp.concatenate([b_one[0, 0], b_one[1, 0], b_two[1, 0], b_two[0, 0]])
    b2 = jnp.concatenate([b_one[0, 1], b_one[1, 1], b_two[1, 1], b_two[0, 1]])
    b3 = jnp.concatenate([b_far[0, 0], b_far[1, 0], b_far[0, 1], b_far[1, 1]])
    early = (w_in, w_out, w_in_p, w_out_p, near_a, near_b, near_a_p, near_b_p)
    early_plan = ((0, 0, 1, 0, SHARD), (2, 0, 3, 0, SHARD)) + tuple((a, 0, a, HALF, HALF) for a in range(4, 8))
    early_bias = jnp.concatenate([b0, b1]).astype(jnp.float32)
    late = (near_a_z, near_b_z, near_a_zp, near_b_zp, far, far_p, far_z, far_zp)
    late_plan = tuple((a, 0, a, HALF, HALF) for a in range(8))
    late_bias = jnp.concatenate([b2, b3]).astype(jnp.float32)

    where = (moved[:, channels].astype(jnp.int32) << 4) + moved[:, channels + 1].astype(jnp.int32)
    onehot = where[None, :] == jnp.arange(cells, dtype=jnp.int32)[:, None]
    placed = jnp.dot(
        onehot.astype(jnp.bfloat16), moved[:, :channels], preferred_element_type=jnp.float32
    )
    present = jnp.any(onehot, axis=1)
    grid = jnp.where(present[:, None], placed, background.astype(jnp.float32)[None, :]).astype(
        jnp.bfloat16
    )
    block = grid.reshape(TH, TW, channels)
    top, bottom = halo(block, "row", 0, 3)
    tall = [
        jnp.concatenate([part[:, cut] for part in (top, block, bottom)], axis=0)
        for cut in (slice(TW - 3, TW), slice(0, 3))
    ]
    ends = lax.axis_size("col") - 1
    left = lax.ppermute(tall[0], "col", [(i, i + 1) for i in range(ends)])
    right = lax.ppermute(tall[1], "col", [(i + 1, i) for i in range(ends)])
    inputs = (block, top, bottom, left, right, conv_weight.reshape(49, channels), conv_bias[None])
    tiles = channels // LANES
    before = conv_call(0, tiles // 2, inputs)
    flat = conv_call(tiles // 2, tiles // 2, inputs, (norm_gain[None], norm_bias[None], before))

    other = send(flat, along_x)
    mine = mlp(flat, early_bias, early, early_plan)
    theirs = mlp(other, early_bias, early, early_plan)
    theirs = mlp(other, late_bias, late, late_plan, acc=theirs, out_dtype=jnp.bfloat16)
    returned = send(theirs, back_x)
    mine = mlp(flat, late_bias, late, late_plan, acc=mine)
    mixed = mine + returned.astype(jnp.float32)
    result = grid.astype(jnp.float32) + layer_scale * (mixed + b_out)
    return result.astype(jnp.bfloat16).reshape(TH, TW, channels)


def solution(mesh):
    placed = (
        P(("row", "col"), None),
        P(("row", "col")),
        P(),
        P(),
        P(),
        P(),
        P(),
        P("col", None),
        P("col"),
        P("col", None),
        P(),
        P(),
    )

    def step(*args):
        return local(*args)

    step = jax.shard_map(
        step, mesh=mesh, in_specs=placed, out_specs=P("row", "col", None), check_vma=False
    )
    return step
```

```python
import functools

import jax
import jax.numpy as jnp
from jax import lax
from jax.experimental import pallas as pl
from jax.experimental.pallas import tpu as pltpu
from jax.sharding import PartitionSpec as P


TH = 32
TW = 16
SHARD = 384
HALF = SHARD // 2
LANES = 128
BAND = TH // 2
PAIRS = BAND // 2
UNITS = 256

VMEM = pltpu.VMEM


def device_index(x, y, z, core):
    x, y, z = x % 4, y % 4, z % 4
    return (z * 2 + x // 2) * 16 + y * 4 + (x % 2) * 2 + core


def routes(move):
    return [
        (device_index(x, y, z, core), device_index(*move(x, y, z, core)))
        for x in range(4)
        for y in range(4)
        for z in range(4)
        for core in range(2)
    ]


def send(value, move):
    return lax.ppermute(value, ("row", "col"), routes(move))


def to_partner(x, y, z, core):
    return x, y, z, 1 - core


def along_y(x, y, z, core):
    return x, y + 1 - 2 * core, z, core


def along_z(x, y, z, core):
    return x, y, z + 1 - 2 * core, core


def along_x(x, y, z, core):
    return x + 1 - 2 * core, y, z, core


def back_x(x, y, z, core):
    return x - 1 + 2 * core, y, z, core


def halo(cells, axis, dim, width):
    count = lax.axis_size(axis)
    ends = count - 1
    head = lax.slice_in_dim(cells, 0, width, axis=dim)
    tail = lax.slice_in_dim(cells, cells.shape[dim] - width, cells.shape[dim], axis=dim)
    return (
        lax.ppermute(tail, axis, [(i, i + 1) for i in range(ends)]),
        lax.ppermute(head, axis, [(i + 1, i) for i in range(ends)]),
    )


def whole(space=VMEM):
    return pl.BlockSpec(memory_space=space)


def stack_kernel(half_ref, *refs):
    *sources, out_ref, sems = refs
    start = pl.multiple_of(half_ref[0] * HALF, HALF)
    copies = [
        pltpu.make_async_copy(source.at[pl.ds(start, HALF)], out_ref.at[pl.ds(k * HALF, HALF)], sems.at[k])
        for k, source in enumerate(sources)
    ]
    for copy in copies:
        copy.start()
    for copy in copies:
        copy.wait()


def stack(half, *sources):
    channels = sources[0].shape[1]
    return pl.pallas_call(
        stack_kernel,
        out_shape=jax.ShapeDtypeStruct((len(sources) * HALF, channels), jnp.bfloat16),
        in_specs=[whole(pltpu.SMEM)] + [whole(pl.ANY)] * len(sources),
        out_specs=whole(),
        scratch_shapes=[pltpu.SemaphoreType.DMA((len(sources),))],
        cost_estimate=pl.CostEstimate(flops=0, bytes_accessed=4 * len(sources) * HALF * channels, transcendentals=0),
        name="stack",
    )(half, *sources)


def conv_kernel(lower, grid_ref, edge_ref, left_ref, right_ref, weight_ref, vector_ref, out_ref, even, odd, both, conv):
    channels = grid_ref.shape[2]
    tiles = channels // LANES
    count = PAIRS + 3

    def tile(t, carry):
        at = pl.ds(pl.multiple_of(t * LANES, LANES), LANES)

        def row(k):
            if lower:
                inside = k < BAND + 3
                middle = grid_ref[TH - BAND - 3 + k, :, at] if inside else edge_ref[k - BAND - 3, :, at]
                side = TH - BAND + k
            else:
                middle = edge_ref[k, :, at] if k < 3 else grid_ref[k - 3, :, at]
                side = k
            parts = (left_ref[side, :, at], middle, right_ref[side, :, at])
            return [part.astype(jnp.float32) for part in parts]

        spans = (slice(5, 8), slice(8, 24), slice(24, 27))
        for k in range(count):
            for span, e, o in zip(spans, row(2 * k), row(2 * k + 1)):
                even[k, span, :] = e
                odd[k, span, :] = o
                both[k, span, :] = e + o
        zero = jnp.zeros((TW, LANES), jnp.float32)
        p, q, s = [zero] * PAIRS, [zero] * (PAIRS + 1), [zero] * PAIRS
        for along in range(7):
            h = [weight_ref[across, along : along + 1, at] for across in range(7)]
            mixed = [h[0]] + [h[2 * j] + h[2 * j - 1] for j in range(1, 4)]
            h, mixed = [[jnp.broadcast_to(v, (TW, LANES)) for v in group] for group in (h, mixed)]
            cols = slice(5 + along, 5 + along + TW)
            for k in range(count):
                e, o, b = even[k, cols, :], odd[k, cols, :], both[k, cols, :]
                for j in range(4):
                    if 0 <= k - j < PAIRS:
                        p[k - j] = p[k - j] + e * h[2 * j]
                        s[k - j] = s[k - j] + b * mixed[j]
                for j in range(3):
                    if 0 <= k - j <= PAIRS:
                        q[k - j] = q[k - j] + o * h[2 * j + 1]
        base = jnp.broadcast_to(vector_ref[0:1, at], (TW, LANES))
        for k in range(PAIRS):
            conv[t, 2 * k * TW : (2 * k + 1) * TW, :] = p[k] + q[k] + base
            conv[t, (2 * k + 1) * TW : (2 * k + 2) * TW, :] = s[k] - p[k] - q[k + 1] + base
        return carry

    lax.fori_loop(0, tiles, tile, 0)

    def norm(b, carry):
        rows = pl.ds(pl.multiple_of(b * 16, 16), 16)
        values = [conv[t, rows, :] for t in range(tiles)]
        mean = jnp.sum(sum(values), axis=-1, keepdims=True) * (1.0 / channels)
        centred = [v - mean for v in values]
        var = jnp.sum(sum(v * v for v in centred), axis=-1, keepdims=True) * (1.0 / channels)
        inverse = lax.rsqrt(var + 1e-06)
        for t in range(tiles):
            at = slice(t * LANES, (t + 1) * LANES)
            out_ref[rows, at] = (centred[t] * inverse * vector_ref[1:2, at] + vector_ref[2:3, at]).astype(
                jnp.bfloat16
            )
        return carry

    lax.fori_loop(0, BAND * TW // 16, norm, 0, unroll=2)


def conv_norm(lower, grid, edge, left, right, weight, vectors):
    channels = grid.shape[2]
    stage = VMEM((PAIRS + 3, 32, LANES), jnp.float32)
    return pl.pallas_call(
        functools.partial(conv_kernel, lower),
        out_shape=jax.ShapeDtypeStruct((BAND * TW, channels), jnp.bfloat16),
        in_specs=[whole()] * 6,
        out_specs=whole(),
        scratch_shapes=[stage, stage, stage, VMEM((channels // LANES, BAND * TW, LANES), jnp.float32)],
        cost_estimate=pl.CostEstimate(
            flops=100 * BAND * TW * channels, bytes_accessed=8 * BAND * TW * channels, transcendentals=0
        ),
        name="conv",
    )(grid, edge, left, right, weight, vectors)


PHI = (
    0.7978849411010742, 0.03633308410644531, -3.259496588725597e-05, -5.5306198191829026e-05,
    3.964745246776147e-06, -1.3226342332472996e-07, 1.7561730958348676e-09,
)


def gelu(pre):
    s = pre * pre
    p = PHI[-1]
    for c in PHI[-2::-1]:
        p = p * s + c
    half = 0.5 * pre
    return half + half * jnp.tanh(pre * p)


def mlp_kernel(plan, bands, count, adds, *refs):
    rows_refs, bias_ref = refs[:bands], refs[bands]
    pieces = refs[bands + 1 : bands + 1 + count]
    acc_ref = refs[bands + 1 + count] if adds else None
    out_ref, rows, w_in, w_out, hid, part, sems, row_sems = refs[bands + 1 + count + adds :]
    blocks = w_in.shape[0] // UNITS
    columns = w_out.shape[1] // UNITS
    ins, outs, at = [], [], 0
    for k, (a, row_a, b, row_b, size) in enumerate(plan):
        ins.append(pltpu.make_async_copy(pieces[a].at[pl.ds(row_a, size)], w_in.at[pl.ds(at, size)], sems.at[k, 0]))
        outs.append(pltpu.make_async_copy(pieces[b].at[pl.ds(row_b, size)], w_out.at[pl.ds(at, size)], sems.at[k, 1]))
        at += size
    step = rows.shape[0] // bands
    moves = [
        pltpu.make_async_copy(ref, rows.at[pl.ds(k * step, step)], row_sems.at[k]) for k, ref in enumerate(rows_refs)
    ]
    early = next(k for k in range(len(plan) + 1) if sum(p[4] for p in plan[:k]) >= 3 * UNITS)
    for copy in moves + ins + outs:
        copy.start()
    for copy in moves + ins[:early]:
        copy.wait()

    def first(h):
        return lax.dot_general(
            rows[...], w_in[h * UNITS : (h + 1) * UNITS, :], (((1,), (1,)), ((), ())),
            preferred_element_type=jnp.float32,
        )

    def middle(h, pre):
        at = slice(h * UNITS, (h + 1) * UNITS)
        hid[:, at] = gelu(pre + bias_ref[0:1, at]).astype(jnp.bfloat16)

    split = blocks // 2 * UNITS

    def second(n, last):
        at = slice(n * UNITS, (n + 1) * UNITS)
        span = slice(split, None) if last else slice(0, split)
        total = jnp.dot(hid[:, span], w_out[span, at], preferred_element_type=jnp.float32)
        if last:
            out_ref[:, at] = (part[:, at] + total).astype(out_ref.dtype)
        else:
            part[:, at] = total + acc_ref[:, at] if adds else total

    waiting, sent = None, 0
    for h in range(blocks):
        if h == blocks // 2:
            for copy in ins[early:] + outs:
                copy.wait()
        pre = first(h)
        if waiting is not None:
            middle(*waiting)
        waiting = (h, pre)
        if h > blocks // 2:
            for n in range(sent, sent + 2):
                second(n, False)
            sent += 2
    middle(*waiting)
    for n in range(sent, columns):
        second(n, False)
    for n in range(columns):
        second(n, True)


def mlp(rows, bias, pieces, plan, acc=None, out_dtype=jnp.float32):
    m, channels = sum(part.shape[0] for part in rows), rows[0].shape[1]
    hidden = sum(p[4] for p in plan)
    adds = acc is not None
    return pl.pallas_call(
        functools.partial(mlp_kernel, plan, len(rows), len(pieces), int(adds)),
        out_shape=jax.ShapeDtypeStruct((m, channels), out_dtype),
        in_specs=[whole(pl.ANY)] * len(rows) + [whole()] + [whole(pl.ANY)] * len(pieces) + [whole()] * adds,
        out_specs=whole(),
        scratch_shapes=[
            VMEM((m, channels), jnp.bfloat16),
            VMEM((hidden, channels), jnp.bfloat16),
            VMEM((hidden, channels), jnp.bfloat16),
            VMEM((m, hidden), jnp.bfloat16),
            VMEM((m, channels), jnp.float32),
            pltpu.SemaphoreType.DMA((len(plan), 2)),
            pltpu.SemaphoreType.DMA((len(rows),)),
        ],
        cost_estimate=pl.CostEstimate(
            flops=4 * m * hidden * channels, bytes_accessed=4 * hidden * channels, transcendentals=m * hidden
        ),
        name="mlp",
    )(*rows, bias.reshape(1, hidden), *pieces, *([acc] if adds else []))


def local(
    patches,
    dest,
    background,
    conv_weight,
    conv_bias,
    norm_gain,
    norm_bias,
    w_in,
    b_in,
    w_out,
    b_out,
    layer_scale,
):
    cells = TH * TW
    channels = patches.shape[1]
    row, col = lax.axis_index("row"), lax.axis_index("col")
    my_y, my_lo, my_core, my_h = col // 4, (col // 2) % 2, col % 2, (row // 2) % 2

    moved = lax.all_to_all(patches, "col", split_axis=0, concat_axis=0, tiled=True)
    slots = dest.reshape(16, 48)
    notes = jnp.concatenate(
        [slots >> 4, slots & 15, jnp.zeros((16, 32), jnp.int32)], axis=1
    ).astype(jnp.bfloat16)
    notes = jnp.concatenate([notes, jnp.broadcast_to(b_in, (16, SHARD))], axis=1)
    notes = lax.all_to_all(notes, "col", split_axis=0, concat_axis=0, tiled=True)

    w_in_p, w_out_p = send(w_in, to_partner), send(w_out, to_partner)
    half = my_h.astype(jnp.int32).reshape(1)
    near_a = send(stack(half, w_in, w_out), along_y)
    near_b = send(stack(half, w_in_p, w_out_p), along_y)
    near_a_z = send(near_a, along_z)
    far = send(near_a, along_y)
    near_a_p = send(near_a, to_partner)
    near_b_z = send(near_b, along_z)
    near_b_p = send(near_b, to_partner)
    far_z = send(far, along_z)
    far_p = send(far, to_partner)
    near_a_zp = send(near_a_z, to_partner)
    near_b_zp = send(near_b_z, to_partner)
    far_zp = send(far_z, to_partner)

    bias = notes[:, 128:].reshape(4, 2, 2, 2, HALF)
    bias = lax.dynamic_index_in_dim(bias, my_lo, axis=1, keepdims=False)
    bias = jnp.where(my_core == 1, bias[:, ::-1], bias)
    turned = jnp.where(my_h == 1, bias[:, :, ::-1], bias)
    ahead = 2 * my_core - 1

    def at(array, step):
        return lax.dynamic_index_in_dim(array, (my_y + step + 4) % 4, axis=0, keepdims=False)

    b_one, b_two, b_far = at(turned, ahead), at(turned, -ahead), at(turned, 2)
    b0 = at(bias, 0).reshape(-1)
    b1 = jnp.concatenate([b_one[0, 0], b_one[1, 0], b_two[1, 0], b_two[0, 0]])
    b2 = jnp.concatenate([b_one[0, 1], b_one[1, 1], b_two[1, 1], b_two[0, 1]])
    b3 = jnp.concatenate([b_far[0, 0], b_far[1, 0], b_far[0, 1], b_far[1, 1]])
    early = (w_in, w_out, w_in_p, w_out_p, near_a, near_b, near_a_p, near_b_p)
    early_plan = ((0, 0, 1, 0, SHARD), (2, 0, 3, 0, SHARD)) + tuple((a, 0, a, HALF, HALF) for a in range(4, 8))
    early_bias = jnp.concatenate([b0, b1]).astype(jnp.float32)
    late = (near_a_z, near_b_z, near_a_zp, near_b_zp, far, far_p, far_z, far_zp)
    late_plan = tuple((a, 0, a, HALF, HALF) for a in range(8))
    late_bias = jnp.concatenate([b2, b3]).astype(jnp.float32)

    where = (notes[:, :48].astype(jnp.int32) << 4) + notes[:, 48:96].astype(jnp.int32)
    where = where.reshape(-1)
    vectors = jnp.stack([conv_bias, norm_gain, norm_bias])
    moved, where, vectors, early_bias, late_bias = lax.optimization_barrier(
        (moved, where, vectors, early_bias, late_bias)
    )
    onehot = where[None, :] == jnp.arange(cells, dtype=jnp.int32)[:, None]
    placed = jnp.dot(
        onehot.astype(jnp.bfloat16), moved, preferred_element_type=jnp.float32
    )
    present = jnp.any(onehot, axis=1)
    grid = jnp.where(present[:, None], placed, background.astype(jnp.float32)[None, :]).astype(
        jnp.bfloat16
    )
    block = grid.reshape(TH, TW, channels)
    top, bottom = halo(block, "row", 0, 3)
    tall = [
        jnp.concatenate([part[:, cut] for part in (top, block, bottom)], axis=0)
        for cut in (slice(TW - 3, TW), slice(0, 3))
    ]
    ends = lax.axis_size("col") - 1
    left = lax.ppermute(tall[0], "col", [(i, i + 1) for i in range(ends)])
    right = lax.ppermute(tall[1], "col", [(i + 1, i) for i in range(ends)])
    flat_a = conv_norm(False, block, top, left, right, conv_weight, vectors)
    flat_b = conv_norm(True, block, bottom, left, right, conv_weight, vectors)

    flat = (flat_a, flat_b)
    other = (send(flat_a, along_x), send(flat_b, along_x))
    mine = mlp(flat, early_bias, early, early_plan)
    theirs = mlp(other, early_bias, early, early_plan)
    theirs = mlp(other, late_bias, late, late_plan, acc=theirs, out_dtype=jnp.bfloat16)
    returned = send(theirs, back_x)
    mine = mlp(flat, late_bias, late, late_plan, acc=mine)
    mixed = mine + returned.astype(jnp.float32)
    result = grid.astype(jnp.float32) + layer_scale * (mixed + b_out)
    return result.astype(jnp.bfloat16).reshape(TH, TW, channels)


def solution(mesh):
    placed = (
        P(("row", "col"), None),
        P(("row", "col")),
        P(),
        P(),
        P(),
        P(),
        P(),
        P("col", None),
        P("col"),
        P("col", None),
        P(),
        P(),
    )

    def step(*args):
        return local(*args)

    step = jax.shard_map(
        step, mesh=mesh, in_specs=placed, out_specs=P("row", "col", None), check_vma=False
    )
    return step
```

```python
import functools

import jax
import jax.numpy as jnp
from jax import lax
from jax.experimental import pallas as pl
from jax.experimental.pallas import tpu as pltpu
from jax.sharding import PartitionSpec as P


TH = 32
TW = 16
SHARD = 384
HALF = SHARD // 2
LANES = 128
BAND = TH // 2
PAIRS = BAND // 2
UNITS = 256

VMEM = pltpu.VMEM


def device_index(x, y, z, core):
    x, y, z = x % 4, y % 4, z % 4
    return (z * 2 + x // 2) * 16 + y * 4 + (x % 2) * 2 + core


def routes(move):
    return [
        (device_index(x, y, z, core), device_index(*move(x, y, z, core)))
        for x in range(4)
        for y in range(4)
        for z in range(4)
        for core in range(2)
    ]


def send(value, move):
    return lax.ppermute(value, ("row", "col"), routes(move))


def to_partner(x, y, z, core):
    return x, y, z, 1 - core


def along_y(x, y, z, core):
    return x, y + 1 - 2 * core, z, core


def along_z(x, y, z, core):
    return x, y, z + 1 - 2 * core, core


def along_x(x, y, z, core):
    return x + 1 - 2 * core, y, z, core


def back_x(x, y, z, core):
    return x - 1 + 2 * core, y, z, core


def halo(cells, axis, dim, width):
    count = lax.axis_size(axis)
    ends = count - 1
    head = lax.slice_in_dim(cells, 0, width, axis=dim)
    tail = lax.slice_in_dim(cells, cells.shape[dim] - width, cells.shape[dim], axis=dim)
    return (
        lax.ppermute(tail, axis, [(i, i + 1) for i in range(ends)]),
        lax.ppermute(head, axis, [(i + 1, i) for i in range(ends)]),
    )


def whole(space=VMEM):
    return pl.BlockSpec(memory_space=space)


def join_kernel(patches_ref, head_ref, out_ref, sem):
    channels = patches_ref.shape[1]
    copy = pltpu.make_async_copy(patches_ref, out_ref.at[:, pl.ds(0, channels)], sem)
    copy.start()
    groups, lines, _ = head_ref.shape
    size = out_ref.shape[0] // groups
    out_ref[:, channels:] = jnp.zeros((out_ref.shape[0], LANES), out_ref.dtype)
    for g in range(groups):
        out_ref[g * size : g * size + lines, channels:] = head_ref[g]
    copy.wait()


def join(patches, head):
    rows, channels = patches.shape
    return pl.pallas_call(
        join_kernel,
        out_shape=jax.ShapeDtypeStruct((rows, channels + LANES), patches.dtype),
        in_specs=[whole(pl.ANY), whole()],
        out_specs=whole(),
        scratch_shapes=[pltpu.SemaphoreType.DMA],
        cost_estimate=pl.CostEstimate(flops=0, bytes_accessed=4 * rows * channels, transcendentals=0),
        name="join",
    )(patches, head)


def stack_kernel(half_ref, *refs):
    *sources, out_ref, sems = refs
    start = pl.multiple_of(half_ref[0] * HALF, HALF)
    copies = [
        pltpu.make_async_copy(source.at[pl.ds(start, HALF)], out_ref.at[pl.ds(k * HALF, HALF)], sems.at[k])
        for k, source in enumerate(sources)
    ]
    for copy in copies:
        copy.start()
    for copy in copies:
        copy.wait()


def stack(half, *sources):
    channels = sources[0].shape[1]
    return pl.pallas_call(
        stack_kernel,
        out_shape=jax.ShapeDtypeStruct((len(sources) * HALF, channels), jnp.bfloat16),
        in_specs=[whole(pltpu.SMEM)] + [whole(pl.ANY)] * len(sources),
        out_specs=whole(),
        scratch_shapes=[pltpu.SemaphoreType.DMA((len(sources),))],
        cost_estimate=pl.CostEstimate(flops=0, bytes_accessed=4 * len(sources) * HALF * channels, transcendentals=0),
        name="stack",
    )(half, *sources)


def notes_kernel(place_ref, moved_ref, slots_ref, bias_ref, notes):
    groups, lines, _ = notes.shape
    notes[...] = moved_ref[:, :lines, moved_ref.shape[2] - LANES :]
    y, lo, core, odd = place_ref[0], place_ref[1], place_ref[2], place_ref[3]
    width = slots_ref.shape[1]
    for g in range(groups):
        parts = notes[g, 0:2, :width].astype(jnp.float32)
        slots_ref[g : g + 1, :] = (parts[0:1] * 16.0 + parts[1:2]).astype(jnp.int32)

    def half(step, other, turn):
        shard = lax.rem(y + step + 4, 4) * 4 + lo * 2 + (1 - core if other else core)
        lines = notes[shard, :, : HALF // 2].astype(jnp.float32)
        one, two = [lines[2:3], lines[3:4]], [lines[4:5], lines[5:6]]
        if turn is None:
            return one + two
        pick = jnp.full(one[0].shape, odd, jnp.int32) == (1 - turn)
        return [jnp.where(pick, q, p) for p, q in zip(one, two)]

    ahead = 2 * core - 1
    early, late = half(0, False, None) + half(0, True, None), []
    for turn, group in ((0, early), (1, late)):
        for step, other in ((ahead, False), (ahead, True), (-ahead, True), (-ahead, False)):
            group += half(step, other, turn)
    for turn, other in ((0, False), (0, True), (1, False), (1, True)):
        late += half(2, other, turn)
    for k, group in enumerate((early, late)):
        for j in range(0, len(group), 4):
            at = slice(j * HALF // 2, (j + 4) * HALF // 2)
            bias_ref[k : k + 1, at] = jnp.concatenate(group[j : j + 4], axis=1)


def read_notes(place, moved):
    groups, width = moved.shape[:2]
    return pl.pallas_call(
        notes_kernel,
        out_shape=[
            jax.ShapeDtypeStruct((groups, width), jnp.int32),
            jax.ShapeDtypeStruct((2, 8 * HALF), jnp.float32),
        ],
        in_specs=[whole(pltpu.SMEM), whole()],
        out_specs=[whole(), whole()],
        scratch_shapes=[VMEM((groups, 8, LANES), jnp.bfloat16)],
        name="notes",
    )(place, moved)


def conv_kernel(lower, grid_ref, edge_ref, left_ref, right_ref, weight_ref, vector_ref, out_ref, even, odd, both, conv):
    channels = grid_ref.shape[2]
    tiles = channels // LANES
    count = PAIRS + 3

    def tile(t, carry):
        at = pl.ds(pl.multiple_of(t * LANES, LANES), LANES)

        def row(k):
            if lower:
                inside = k < BAND + 3
                middle = grid_ref[TH - BAND - 3 + k, :, at] if inside else edge_ref[k - BAND - 3, :, at]
                side = TH - BAND + k
            else:
                middle = edge_ref[k, :, at] if k < 3 else grid_ref[k - 3, :, at]
                side = k
            parts = (left_ref[side, :, at], middle, right_ref[side, :, at])
            return [part.astype(jnp.float32) for part in parts]

        spans = (slice(5, 8), slice(8, 24), slice(24, 27))
        for k in range(count):
            for span, e, o in zip(spans, row(2 * k), row(2 * k + 1)):
                even[k, span, :] = e
                odd[k, span, :] = o
                both[k, span, :] = e + o
        zero = jnp.zeros((TW, LANES), jnp.float32)
        p, q, s = [zero] * PAIRS, [zero] * (PAIRS + 1), [zero] * PAIRS
        for along in range(7):
            h = [weight_ref[across, along : along + 1, at] for across in range(7)]
            mixed = [h[0]] + [h[2 * j] + h[2 * j - 1] for j in range(1, 4)]
            h, mixed = [[jnp.broadcast_to(v, (TW, LANES)) for v in group] for group in (h, mixed)]
            cols = slice(5 + along, 5 + along + TW)
            for k in range(count):
                e, o, b = even[k, cols, :], odd[k, cols, :], both[k, cols, :]
                for j in range(4):
                    if 0 <= k - j < PAIRS:
                        p[k - j] = p[k - j] + e * h[2 * j]
                        s[k - j] = s[k - j] + b * mixed[j]
                for j in range(3):
                    if 0 <= k - j <= PAIRS:
                        q[k - j] = q[k - j] + o * h[2 * j + 1]
        base = jnp.broadcast_to(vector_ref[0:1, at], (TW, LANES))
        for k in range(PAIRS):
            conv[t, 2 * k * TW : (2 * k + 1) * TW, :] = p[k] + q[k] + base
            conv[t, (2 * k + 1) * TW : (2 * k + 2) * TW, :] = s[k] - p[k] - q[k + 1] + base
        return carry

    lax.fori_loop(0, tiles, tile, 0)

    def norm(b, carry):
        rows = pl.ds(pl.multiple_of(b * 16, 16), 16)
        values = [conv[t, rows, :] for t in range(tiles)]
        mean = jnp.sum(sum(values), axis=-1, keepdims=True) * (1.0 / channels)
        centred = [v - mean for v in values]
        var = jnp.sum(sum(v * v for v in centred), axis=-1, keepdims=True) * (1.0 / channels)
        inverse = lax.rsqrt(var + 1e-06)
        for t in range(tiles):
            at = slice(t * LANES, (t + 1) * LANES)
            out_ref[rows, at] = (centred[t] * inverse * vector_ref[1:2, at] + vector_ref[2:3, at]).astype(
                jnp.bfloat16
            )
        return carry

    lax.fori_loop(0, BAND * TW // 16, norm, 0, unroll=2)


def conv_norm(lower, grid, edge, left, right, weight, vectors):
    channels = grid.shape[2]
    stage = VMEM((PAIRS + 3, 32, LANES), jnp.float32)
    return pl.pallas_call(
        functools.partial(conv_kernel, lower),
        out_shape=jax.ShapeDtypeStruct((BAND * TW, channels), jnp.bfloat16),
        in_specs=[whole()] * 6,
        out_specs=whole(),
        scratch_shapes=[stage, stage, stage, VMEM((channels // LANES, BAND * TW, LANES), jnp.float32)],
        cost_estimate=pl.CostEstimate(
            flops=100 * BAND * TW * channels, bytes_accessed=8 * BAND * TW * channels, transcendentals=0
        ),
        name="conv",
    )(grid, edge, left, right, weight, vectors)


PHI = (
    0.7978849411010742, 0.03633308410644531, -3.259496588725597e-05, -5.5306198191829026e-05,
    3.964745246776147e-06, -1.3226342332472996e-07, 1.7561730958348676e-09,
)


def gelu(pre):
    s = pre * pre
    p = PHI[-1]
    for c in PHI[-2::-1]:
        p = p * s + c
    half = 0.5 * pre
    return half + half * jnp.tanh(pre * p)


def mlp_kernel(plan, line, bands, count, adds, *refs):
    rows_refs, bias_ref = refs[:bands], refs[bands]
    pieces = refs[bands + 1 : bands + 1 + count]
    acc_ref = refs[bands + 1 + count] if adds else None
    out_ref, rows, w_in, w_out, hid, sems, row_sems = refs[bands + 1 + count + adds :]
    blocks = w_in.shape[0] // UNITS
    columns = w_out.shape[1] // UNITS
    ins, outs, at = [], [], 0
    for k, (a, row_a, b, row_b, size) in enumerate(plan):
        ins.append(pltpu.make_async_copy(pieces[a].at[pl.ds(row_a, size)], w_in.at[pl.ds(at, size)], sems.at[k, 0]))
        outs.append(pltpu.make_async_copy(pieces[b].at[pl.ds(row_b, size)], w_out.at[pl.ds(at, size)], sems.at[k, 1]))
        at += size
    step = rows.shape[0] // bands
    moves = [
        pltpu.make_async_copy(ref, rows.at[pl.ds(k * step, step)], row_sems.at[k]) for k, ref in enumerate(rows_refs)
    ]
    early = next(k for k in range(len(plan) + 1) if sum(p[4] for p in plan[:k]) >= 3 * UNITS)
    for copy in moves + ins + outs:
        copy.start()
    for copy in moves + ins[:early]:
        copy.wait()

    def first(h):
        return lax.dot_general(
            rows[...], w_in[h * UNITS : (h + 1) * UNITS, :], (((1,), (1,)), ((), ())),
            preferred_element_type=jnp.float32,
        )

    def middle(h, pre):
        at = slice(h * UNITS, (h + 1) * UNITS)
        hid[:, at] = gelu(pre + bias_ref[line : line + 1, at]).astype(jnp.bfloat16)

    waiting = None
    for h in range(blocks):
        if h == blocks // 2:
            for copy in ins[early:] + outs:
                copy.wait()
        pre = first(h)
        if waiting is not None:
            middle(*waiting)
        waiting = (h, pre)
    middle(*waiting)
    for n in range(columns):
        at = slice(n * UNITS, (n + 1) * UNITS)
        total = jnp.dot(hid[...], w_out[:, at], preferred_element_type=jnp.float32)
        if adds:
            total = total + acc_ref[:, at]
        out_ref[:, at] = total.astype(out_ref.dtype)


def mlp(rows, bias, line, pieces, plan, acc=None, out_dtype=jnp.float32):
    m, channels = sum(part.shape[0] for part in rows), rows[0].shape[1]
    hidden = sum(p[4] for p in plan)
    adds = acc is not None
    return pl.pallas_call(
        functools.partial(mlp_kernel, plan, line, len(rows), len(pieces), int(adds)),
        out_shape=jax.ShapeDtypeStruct((m, channels), out_dtype),
        in_specs=[whole(pl.ANY)] * len(rows) + [whole()] + [whole(pl.ANY)] * len(pieces) + [whole()] * adds,
        out_specs=whole(),
        scratch_shapes=[
            VMEM((m, channels), jnp.bfloat16),
            VMEM((hidden, channels), jnp.bfloat16),
            VMEM((hidden, channels), jnp.bfloat16),
            VMEM((m, hidden), jnp.bfloat16),
            pltpu.SemaphoreType.DMA((len(plan), 2)),
            pltpu.SemaphoreType.DMA((len(rows),)),
        ],
        cost_estimate=pl.CostEstimate(
            flops=4 * m * hidden * channels, bytes_accessed=4 * hidden * channels, transcendentals=m * hidden
        ),
        name="mlp",
    )(*rows, bias, *pieces, *([acc] if adds else []))


def local(
    patches,
    dest,
    background,
    conv_weight,
    conv_bias,
    norm_gain,
    norm_bias,
    w_in,
    b_in,
    w_out,
    b_out,
    layer_scale,
):
    cells = TH * TW
    channels = patches.shape[1]
    row, col = lax.axis_index("row"), lax.axis_index("col")
    my_y, my_lo, my_core, my_h = col // 4, (col // 2) % 2, col % 2, (row // 2) % 2

    slots = dest.reshape(16, 1, 48)
    parts = jnp.concatenate([slots >> 4, slots & 15], axis=1).astype(jnp.bfloat16)
    ours = jnp.broadcast_to(b_in.reshape(1, 4, HALF // 2), (16, 4, HALF // 2))
    head = jnp.concatenate(
        [jnp.pad(parts, ((0, 0), (0, 0), (0, 80))), jnp.pad(ours, ((0, 0), (0, 2), (0, 32)))], axis=1
    )
    moved = lax.all_to_all(join(patches, head), "col", split_axis=0, concat_axis=0, tiled=True)

    half = my_h.astype(jnp.int32).reshape(1)
    near_a = send(stack(half, w_in, w_out), along_y)
    w_in_p, w_out_p = send(w_in, to_partner), send(w_out, to_partner)
    near_b = send(stack(half, w_in_p, w_out_p), along_y)
    near_a_z = send(near_a, along_z)
    far = send(near_a, along_y)
    near_a_p = send(near_a, to_partner)
    near_b_z = send(near_b, along_z)
    near_b_p = send(near_b, to_partner)
    far_z = send(far, along_z)
    far_p = send(far, to_partner)
    near_a_zp = send(near_a_z, to_partner)
    near_b_zp = send(near_b_z, to_partner)
    far_zp = send(far_z, to_partner)

    early = (w_in, w_out, w_in_p, w_out_p, near_a, near_b, near_a_p, near_b_p)
    early_plan = ((0, 0, 1, 0, SHARD), (2, 0, 3, 0, SHARD)) + tuple((a, 0, a, HALF, HALF) for a in range(4, 8))
    late = (near_a_z, near_b_z, near_a_zp, near_b_zp, far, far_p, far_z, far_zp)
    late_plan = tuple((a, 0, a, HALF, HALF) for a in range(8))

    place = jnp.stack([my_y, my_lo, my_core, my_h]).astype(jnp.int32)
    vectors = jnp.stack([conv_bias, norm_gain, norm_bias])
    moved, vectors, place = lax.optimization_barrier((moved, vectors, place))
    where, bias = read_notes(place, moved.reshape(16, 48, -1))
    where = where.reshape(-1)
    onehot = where[None, :] == jnp.arange(cells, dtype=jnp.int32)[:, None]
    placed = jnp.dot(
        onehot.astype(jnp.bfloat16), moved[:, :channels], preferred_element_type=jnp.float32
    )
    present = jnp.any(onehot, axis=1)
    grid = jnp.where(present[:, None], placed, background.astype(jnp.float32)[None, :]).astype(
        jnp.bfloat16
    )
    block = grid.reshape(TH, TW, channels)
    top, bottom = halo(block, "row", 0, 3)
    tall = [
        jnp.concatenate([part[:, cut] for part in (top, block, bottom)], axis=0)
        for cut in (slice(TW - 3, TW), slice(0, 3))
    ]
    ends = lax.axis_size("col") - 1
    left = lax.ppermute(tall[0], "col", [(i, i + 1) for i in range(ends)])
    right = lax.ppermute(tall[1], "col", [(i + 1, i) for i in range(ends)])
    flat_a = conv_norm(False, block, top, left, right, conv_weight, vectors)
    flat_b = conv_norm(True, block, bottom, left, right, conv_weight, vectors)

    flat = (flat_a, flat_b)
    other = (send(flat_a, along_x), send(flat_b, along_x))
    mine = mlp(flat, bias, 0, early, early_plan)
    theirs = mlp(other, bias, 0, early, early_plan)
    theirs = mlp(other, bias, 1, late, late_plan, acc=theirs, out_dtype=jnp.bfloat16)
    returned = send(theirs, back_x)
    mine = mlp(flat, bias, 1, late, late_plan, acc=mine)
    mixed = mine + returned.astype(jnp.float32)
    result = grid.astype(jnp.float32) + layer_scale * (mixed + b_out)
    return result.astype(jnp.bfloat16).reshape(TH, TW, channels)


def solution(mesh):
    placed = (
        P(("row", "col"), None),
        P(("row", "col")),
        P(),
        P(),
        P(),
        P(),
        P(),
        P("col", None),
        P("col"),
        P("col", None),
        P(),
        P(),
    )

    def step(*args):
        return local(*args)

    step = jax.shard_map(
        step, mesh=mesh, in_specs=placed, out_specs=P("row", "col", None), check_vma=False
    )
    return step
```

```python
import functools

import jax
import jax.numpy as jnp
from jax import lax
from jax.experimental import pallas as pl
from jax.experimental.pallas import tpu as pltpu
from jax.sharding import PartitionSpec as P


TH = 32
TW = 16
SHARD = 384
HALF = SHARD // 2
LANES = 128
BAND = TH // 2
PAIRS = BAND // 2
UNITS = 256

VMEM = pltpu.VMEM


def device_index(x, y, z, core):
    x, y, z = x % 4, y % 4, z % 4
    return (z * 2 + x // 2) * 16 + y * 4 + (x % 2) * 2 + core


def routes(move):
    return [
        (device_index(x, y, z, core), device_index(*move(x, y, z, core)))
        for x in range(4)
        for y in range(4)
        for z in range(4)
        for core in range(2)
    ]


def send(value, move):
    return lax.ppermute(value, ("row", "col"), routes(move))


def to_partner(x, y, z, core):
    return x, y, z, 1 - core


def along_y(x, y, z, core):
    return x, y + 1 - 2 * core, z, core


def along_z(x, y, z, core):
    return x, y, z + 1 - 2 * core, core


def along_x(x, y, z, core):
    return x + 1 - 2 * core, y, z, core


def back_x(x, y, z, core):
    return x - 1 + 2 * core, y, z, core


def halo(cells, axis, dim, width):
    count = lax.axis_size(axis)
    ends = count - 1
    head = lax.slice_in_dim(cells, 0, width, axis=dim)
    tail = lax.slice_in_dim(cells, cells.shape[dim] - width, cells.shape[dim], axis=dim)
    return (
        lax.ppermute(tail, axis, [(i, i + 1) for i in range(ends)]),
        lax.ppermute(head, axis, [(i + 1, i) for i in range(ends)]),
    )


def whole(space=VMEM):
    return pl.BlockSpec(memory_space=space)


def grant(mib):
    return pltpu.CompilerParams(vmem_limit_bytes=mib * 1024 * 1024)


def join_kernel(patches_ref, head_ref, out_ref, sem):
    channels = patches_ref.shape[1]
    copy = pltpu.make_async_copy(patches_ref, out_ref.at[:, pl.ds(0, channels)], sem)
    copy.start()
    groups, lines, _ = head_ref.shape
    size = out_ref.shape[0] // groups
    out_ref[:, channels:] = jnp.zeros((out_ref.shape[0], LANES), out_ref.dtype)
    for g in range(groups):
        out_ref[g * size : g * size + lines, channels:] = head_ref[g]
    copy.wait()


def join(patches, head):
    rows, channels = patches.shape
    return pl.pallas_call(
        join_kernel,
        out_shape=jax.ShapeDtypeStruct((rows, channels + LANES), patches.dtype),
        in_specs=[whole(pl.ANY), whole()],
        out_specs=whole(),
        scratch_shapes=[pltpu.SemaphoreType.DMA],
        cost_estimate=pl.CostEstimate(flops=0, bytes_accessed=4 * rows * channels, transcendentals=0),
        compiler_params=grant(7),
        name="join",
    )(patches, head)


def stack_kernel(half_ref, *refs):
    *sources, out_ref, sems = refs
    start = pl.multiple_of(half_ref[0] * HALF, HALF)
    copies = [
        pltpu.make_async_copy(source.at[pl.ds(start, HALF)], out_ref.at[pl.ds(k * HALF, HALF)], sems.at[k])
        for k, source in enumerate(sources)
    ]
    for copy in copies:
        copy.start()
    for copy in copies:
        copy.wait()


def stack(half, *sources):
    channels = sources[0].shape[1]
    return pl.pallas_call(
        stack_kernel,
        out_shape=jax.ShapeDtypeStruct((len(sources) * HALF, channels), jnp.bfloat16),
        in_specs=[whole(pltpu.SMEM)] + [whole(pl.ANY)] * len(sources),
        out_specs=whole(),
        scratch_shapes=[pltpu.SemaphoreType.DMA((len(sources),))],
        cost_estimate=pl.CostEstimate(flops=0, bytes_accessed=4 * len(sources) * HALF * channels, transcendentals=0),
        compiler_params=grant(4),
        name="stack",
    )(half, *sources)


def notes_kernel(place_ref, moved_ref, slots_ref, bias_ref, notes):
    groups, lines, _ = notes.shape
    notes[...] = moved_ref[:, :lines, moved_ref.shape[2] - LANES :]
    y, lo, core, odd = place_ref[0], place_ref[1], place_ref[2], place_ref[3]
    width = slots_ref.shape[1]
    for g in range(groups):
        parts = notes[g, 0:2, :width].astype(jnp.float32)
        slots_ref[g : g + 1, :] = (parts[0:1] * 16.0 + parts[1:2]).astype(jnp.int32)

    def half(step, other, turn):
        shard = lax.rem(y + step + 4, 4) * 4 + lo * 2 + (1 - core if other else core)
        lines = notes[shard, :, : HALF // 2].astype(jnp.float32)
        one, two = [lines[2:3], lines[3:4]], [lines[4:5], lines[5:6]]
        if turn is None:
            return one + two
        pick = jnp.full(one[0].shape, odd, jnp.int32) == (1 - turn)
        return [jnp.where(pick, q, p) for p, q in zip(one, two)]

    ahead = 2 * core - 1
    early, late = half(0, False, None) + half(0, True, None), []
    for turn, group in ((0, early), (1, late)):
        for step, other in ((ahead, False), (ahead, True), (-ahead, True), (-ahead, False)):
            group += half(step, other, turn)
    for turn, other in ((0, False), (0, True), (1, False), (1, True)):
        late += half(2, other, turn)
    for k, group in enumerate((early, late)):
        for j in range(0, len(group), 4):
            at = slice(j * HALF // 2, (j + 4) * HALF // 2)
            bias_ref[k : k + 1, at] = jnp.concatenate(group[j : j + 4], axis=1)


def read_notes(place, moved):
    groups, width = moved.shape[:2]
    return pl.pallas_call(
        notes_kernel,
        out_shape=[
            jax.ShapeDtypeStruct((groups, width), jnp.int32),
            jax.ShapeDtypeStruct((2, 8 * HALF), jnp.float32),
        ],
        in_specs=[whole(pltpu.SMEM), whole()],
        out_specs=[whole(), whole()],
        scratch_shapes=[VMEM((groups, 8, LANES), jnp.bfloat16)],
        compiler_params=grant(7),
        name="notes",
    )(place, moved)


def conv_kernel(lower, grid_ref, edge_ref, left_ref, right_ref, weight_ref, vector_ref, out_ref, even, odd, both, conv):
    channels = grid_ref.shape[2]
    tiles = channels // LANES
    count = PAIRS + 3

    def tile(t, carry):
        at = pl.ds(pl.multiple_of(t * LANES, LANES), LANES)

        def row(k):
            if lower:
                inside = k < BAND + 3
                middle = grid_ref[TH - BAND - 3 + k, :, at] if inside else edge_ref[k - BAND - 3, :, at]
                side = TH - BAND + k
            else:
                middle = edge_ref[k, :, at] if k < 3 else grid_ref[k - 3, :, at]
                side = k
            parts = (left_ref[side, :, at], middle, right_ref[side, :, at])
            return [part.astype(jnp.float32) for part in parts]

        spans = (slice(5, 8), slice(8, 24), slice(24, 27))
        for k in range(count):
            for span, e, o in zip(spans, row(2 * k), row(2 * k + 1)):
                even[k, span, :] = e
                odd[k, span, :] = o
                both[k, span, :] = e + o
        zero = jnp.zeros((TW, LANES), jnp.float32)
        p, q, s = [zero] * PAIRS, [zero] * (PAIRS + 1), [zero] * PAIRS
        for along in range(7):
            h = [weight_ref[across, along : along + 1, at] for across in range(7)]
            mixed = [h[0]] + [h[2 * j] + h[2 * j - 1] for j in range(1, 4)]
            h, mixed = [[jnp.broadcast_to(v, (TW, LANES)) for v in group] for group in (h, mixed)]
            cols = slice(5 + along, 5 + along + TW)
            for k in range(count):
                e, o, b = even[k, cols, :], odd[k, cols, :], both[k, cols, :]
                for j in range(4):
                    if 0 <= k - j < PAIRS:
                        p[k - j] = p[k - j] + e * h[2 * j]
                        s[k - j] = s[k - j] + b * mixed[j]
                for j in range(3):
                    if 0 <= k - j <= PAIRS:
                        q[k - j] = q[k - j] + o * h[2 * j + 1]
        base = jnp.broadcast_to(vector_ref[0:1, at], (TW, LANES))
        for k in range(PAIRS):
            conv[t, 2 * k * TW : (2 * k + 1) * TW, :] = p[k] + q[k] + base
            conv[t, (2 * k + 1) * TW : (2 * k + 2) * TW, :] = s[k] - p[k] - q[k + 1] + base
        return carry

    lax.fori_loop(0, tiles, tile, 0)

    def norm(b, carry):
        rows = pl.ds(pl.multiple_of(b * 16, 16), 16)
        values = [conv[t, rows, :] for t in range(tiles)]
        mean = jnp.sum(sum(values), axis=-1, keepdims=True) * (1.0 / channels)
        centred = [v - mean for v in values]
        var = jnp.sum(sum(v * v for v in centred), axis=-1, keepdims=True) * (1.0 / channels)
        inverse = lax.rsqrt(var + 1e-06)
        for t in range(tiles):
            at = slice(t * LANES, (t + 1) * LANES)
            out_ref[rows, at] = (centred[t] * inverse * vector_ref[1:2, at] + vector_ref[2:3, at]).astype(
                jnp.bfloat16
            )
        return carry

    lax.fori_loop(0, BAND * TW // 16, norm, 0, unroll=2)


def conv_norm(lower, grid, edge, left, right, weight, vectors):
    channels = grid.shape[2]
    stage = VMEM((PAIRS + 3, 32, LANES), jnp.float32)
    return pl.pallas_call(
        functools.partial(conv_kernel, lower),
        out_shape=jax.ShapeDtypeStruct((BAND * TW, channels), jnp.bfloat16),
        in_specs=[whole()] * 6,
        out_specs=whole(),
        scratch_shapes=[stage, stage, stage, VMEM((channels // LANES, BAND * TW, LANES), jnp.float32)],
        cost_estimate=pl.CostEstimate(
            flops=100 * BAND * TW * channels, bytes_accessed=8 * BAND * TW * channels, transcendentals=0
        ),
        compiler_params=grant(14),
        name="conv",
    )(grid, edge, left, right, weight, vectors)


PHI = (
    0.7978849411010742, 0.03633308410644531, -3.259496588725597e-05, -5.5306198191829026e-05,
    3.964745246776147e-06, -1.3226342332472996e-07, 1.7561730958348676e-09,
)


def gelu(pre):
    s = pre * pre
    p = PHI[-1]
    for c in PHI[-2::-1]:
        p = p * s + c
    half = 0.5 * pre
    return half + half * jnp.tanh(pre * p)


def mlp_kernel(plan, line, bands, count, adds, *refs):
    rows_refs, bias_ref = refs[:bands], refs[bands]
    pieces = refs[bands + 1 : bands + 1 + count]
    acc_ref = refs[bands + 1 + count] if adds else None
    out_ref, rows, w_in, w_out, hid, sems, row_sems = refs[bands + 1 + count + adds :]
    blocks = w_in.shape[0] // UNITS
    columns = w_out.shape[1] // UNITS
    ins, outs, at = [], [], 0
    for k, (a, row_a, b, row_b, size) in enumerate(plan):
        ins.append(pltpu.make_async_copy(pieces[a].at[pl.ds(row_a, size)], w_in.at[pl.ds(at, size)], sems.at[k, 0]))
        outs.append(pltpu.make_async_copy(pieces[b].at[pl.ds(row_b, size)], w_out.at[pl.ds(at, size)], sems.at[k, 1]))
        at += size
    step = rows.shape[0] // bands
    moves = [
        pltpu.make_async_copy(ref, rows.at[pl.ds(k * step, step)], row_sems.at[k]) for k, ref in enumerate(rows_refs)
    ]
    early = next(k for k in range(len(plan) + 1) if sum(p[4] for p in plan[:k]) >= 3 * UNITS)
    for copy in moves + ins + outs:
        copy.start()
    for copy in moves + ins[:early]:
        copy.wait()

    def first(h):
        return lax.dot_general(
            rows[...], w_in[h * UNITS : (h + 1) * UNITS, :], (((1,), (1,)), ((), ())),
            preferred_element_type=jnp.float32,
        )

    def middle(h, pre):
        at = slice(h * UNITS, (h + 1) * UNITS)
        hid[:, at] = gelu(pre + bias_ref[line : line + 1, at]).astype(jnp.bfloat16)

    waiting = None
    for h in range(blocks):
        if h == blocks // 2:
            for copy in ins[early:] + outs:
                copy.wait()
        pre = first(h)
        if waiting is not None:
            middle(*waiting)
        waiting = (h, pre)
    middle(*waiting)
    for n in range(columns):
        at = slice(n * UNITS, (n + 1) * UNITS)
        total = jnp.dot(hid[...], w_out[:, at], preferred_element_type=jnp.float32)
        if adds:
            total = total + acc_ref[:, at]
        out_ref[:, at] = total.astype(out_ref.dtype)


def mlp(rows, bias, line, pieces, plan, acc=None, out_dtype=jnp.float32):
    m, channels = sum(part.shape[0] for part in rows), rows[0].shape[1]
    hidden = sum(p[4] for p in plan)
    adds = acc is not None
    return pl.pallas_call(
        functools.partial(mlp_kernel, plan, line, len(rows), len(pieces), int(adds)),
        out_shape=jax.ShapeDtypeStruct((m, channels), out_dtype),
        in_specs=[whole(pl.ANY)] * len(rows) + [whole()] + [whole(pl.ANY)] * len(pieces) + [whole()] * adds,
        out_specs=whole(),
        scratch_shapes=[
            VMEM((m, channels), jnp.bfloat16),
            VMEM((hidden, channels), jnp.bfloat16),
            VMEM((hidden, channels), jnp.bfloat16),
            VMEM((m, hidden), jnp.bfloat16),
            pltpu.SemaphoreType.DMA((len(plan), 2)),
            pltpu.SemaphoreType.DMA((len(rows),)),
        ],
        cost_estimate=pl.CostEstimate(
            flops=4 * m * hidden * channels, bytes_accessed=4 * hidden * channels, transcendentals=m * hidden
        ),
        compiler_params=grant(28),
        name="mlp",
    )(*rows, bias, *pieces, *([acc] if adds else []))


def local(
    patches,
    dest,
    background,
    conv_weight,
    conv_bias,
    norm_gain,
    norm_bias,
    w_in,
    b_in,
    w_out,
    b_out,
    layer_scale,
):
    cells = TH * TW
    channels = patches.shape[1]
    row, col = lax.axis_index("row"), lax.axis_index("col")
    my_y, my_lo, my_core, my_h = col // 4, (col // 2) % 2, col % 2, (row // 2) % 2

    slots = dest.reshape(16, 1, 48)
    parts = jnp.concatenate([slots >> 4, slots & 15], axis=1).astype(jnp.bfloat16)
    ours = jnp.broadcast_to(b_in.reshape(1, 4, HALF // 2), (16, 4, HALF // 2))
    head = jnp.concatenate(
        [jnp.pad(parts, ((0, 0), (0, 0), (0, 80))), jnp.pad(ours, ((0, 0), (0, 2), (0, 32)))], axis=1
    )
    moved = lax.all_to_all(join(patches, head), "col", split_axis=0, concat_axis=0, tiled=True)

    half = my_h.astype(jnp.int32).reshape(1)
    near_a = send(stack(half, w_in, w_out), along_y)
    w_in_p, w_out_p = send(w_in, to_partner), send(w_out, to_partner)
    near_b = send(stack(half, w_in_p, w_out_p), along_y)
    near_a_z = send(near_a, along_z)
    far = send(near_a, along_y)
    near_a_p = send(near_a, to_partner)
    near_b_z = send(near_b, along_z)
    near_b_p = send(near_b, to_partner)
    far_z = send(far, along_z)
    far_p = send(far, to_partner)
    near_a_zp = send(near_a_z, to_partner)
    near_b_zp = send(near_b_z, to_partner)
    far_zp = send(far_z, to_partner)

    early = (w_in, w_out, w_in_p, w_out_p, near_a, near_b, near_a_p, near_b_p)
    early_plan = ((0, 0, 1, 0, SHARD), (2, 0, 3, 0, SHARD)) + tuple((a, 0, a, HALF, HALF) for a in range(4, 8))
    late = (near_a_z, near_b_z, near_a_zp, near_b_zp, far, far_p, far_z, far_zp)
    late_plan = tuple((a, 0, a, HALF, HALF) for a in range(8))

    place = jnp.stack([my_y, my_lo, my_core, my_h]).astype(jnp.int32)
    vectors = jnp.stack([conv_bias, norm_gain, norm_bias])
    moved, vectors, place = lax.optimization_barrier((moved, vectors, place))
    where, bias = read_notes(place, moved.reshape(16, 48, -1))
    where = where.reshape(-1)
    onehot = where[None, :] == jnp.arange(cells, dtype=jnp.int32)[:, None]
    placed = jnp.dot(
        onehot.astype(jnp.bfloat16), moved[:, :channels], preferred_element_type=jnp.float32
    )
    present = jnp.any(onehot, axis=1)
    grid = jnp.where(present[:, None], placed, background.astype(jnp.float32)[None, :]).astype(
        jnp.bfloat16
    )
    block = grid.reshape(TH, TW, channels)
    top, bottom = halo(block, "row", 0, 3)
    tall = [
        jnp.concatenate([part[:, cut] for part in (top, block, bottom)], axis=0)
        for cut in (slice(TW - 3, TW), slice(0, 3))
    ]
    ends = lax.axis_size("col") - 1
    left = lax.ppermute(tall[0], "col", [(i, i + 1) for i in range(ends)])
    right = lax.ppermute(tall[1], "col", [(i + 1, i) for i in range(ends)])
    flat_a = conv_norm(False, block, top, left, right, conv_weight, vectors)
    flat_b = conv_norm(True, block, bottom, left, right, conv_weight, vectors)

    flat = (flat_a, flat_b)
    other = (send(flat_a, along_x), send(flat_b, along_x))
    mine = mlp(flat, bias, 0, early, early_plan)
    theirs = mlp(other, bias, 0, early, early_plan)
    theirs = mlp(other, bias, 1, late, late_plan, acc=theirs, out_dtype=jnp.bfloat16)
    returned = send(theirs, back_x)
    mine = mlp(flat, bias, 1, late, late_plan, acc=mine)
    mixed = mine + returned.astype(jnp.float32)
    result = grid.astype(jnp.float32) + layer_scale * (mixed + b_out)
    return result.astype(jnp.bfloat16).reshape(TH, TW, channels)


def solution(mesh):
    placed = (
        P(("row", "col"), None),
        P(("row", "col")),
        P(),
        P(),
        P(),
        P(),
        P(),
        P("col", None),
        P("col"),
        P("col", None),
        P(),
        P(),
    )

    def step(*args):
        return local(*args)

    step = jax.shard_map(
        step, mesh=mesh, in_specs=placed, out_specs=P("row", "col", None), check_vma=False
    )
    return step
```

```python
import functools

import jax
import jax.numpy as jnp
from jax import lax
from jax.experimental import pallas as pl
from jax.experimental.pallas import tpu as pltpu
from jax.sharding import PartitionSpec as P


TH = 32
TW = 16
SHARD = 384
HALF = SHARD // 2
LANES = 128
HALO = 3
MIDDLE = ((8, 16),)
EDGES = ((0, 8), (24, 8))
UNITS = 256

VMEM = pltpu.VMEM


def device_index(x, y, z, core):
    x, y, z = x % 4, y % 4, z % 4
    return (z * 2 + x // 2) * 16 + y * 4 + (x % 2) * 2 + core


def routes(move):
    return [
        (device_index(x, y, z, core), device_index(*move(x, y, z, core)))
        for x in range(4)
        for y in range(4)
        for z in range(4)
        for core in range(2)
    ]


def send(value, move):
    return lax.ppermute(value, ("row", "col"), routes(move))


def to_partner(x, y, z, core):
    return x, y, z, 1 - core


def along_y(x, y, z, core):
    return x, y + 1 - 2 * core, z, core


def along_z(x, y, z, core):
    return x, y, z + 1 - 2 * core, core


def along_x(x, y, z, core):
    return x + 1 - 2 * core, y, z, core


def back_x(x, y, z, core):
    return x - 1 + 2 * core, y, z, core


def shift(value, axis, step):
    last = lax.axis_size(axis) - 1
    pairs = [(i, i + 1) if step > 0 else (i + 1, i) for i in range(last)]
    return lax.ppermute(value, axis, pairs)


def whole(space=VMEM):
    return pl.BlockSpec(memory_space=space)


def grant(mib):
    return pltpu.CompilerParams(vmem_limit_bytes=mib * 1024 * 1024)


def join_kernel(patches_ref, head_ref, out_ref, sem):
    channels = patches_ref.shape[1]
    copy = pltpu.make_async_copy(patches_ref, out_ref.at[:, pl.ds(0, channels)], sem)
    copy.start()
    groups, lines, _ = head_ref.shape
    size = out_ref.shape[0] // groups
    out_ref[:, channels:] = jnp.zeros((out_ref.shape[0], LANES), out_ref.dtype)
    for g in range(groups):
        out_ref[g * size : g * size + lines, channels:] = head_ref[g]
    copy.wait()


def join(patches, head):
    rows, channels = patches.shape
    return pl.pallas_call(
        join_kernel,
        out_shape=jax.ShapeDtypeStruct((rows, channels + LANES), patches.dtype),
        in_specs=[whole(pl.ANY), whole()],
        out_specs=whole(),
        scratch_shapes=[pltpu.SemaphoreType.DMA],
        cost_estimate=pl.CostEstimate(flops=0, bytes_accessed=4 * rows * channels, transcendentals=0),
        compiler_params=grant(7),
        name="join",
    )(patches, head)


def stack_kernel(half_ref, *refs):
    *sources, out_ref, sems = refs
    start = pl.multiple_of(half_ref[0] * HALF, HALF)
    copies = [
        pltpu.make_async_copy(source.at[pl.ds(start, HALF)], out_ref.at[pl.ds(k * HALF, HALF)], sems.at[k])
        for k, source in enumerate(sources)
    ]
    for copy in copies:
        copy.start()
    for copy in copies:
        copy.wait()


def stack(half, *sources):
    channels = sources[0].shape[1]
    return pl.pallas_call(
        stack_kernel,
        out_shape=jax.ShapeDtypeStruct((len(sources) * HALF, channels), jnp.bfloat16),
        in_specs=[whole(pltpu.SMEM)] + [whole(pl.ANY)] * len(sources),
        out_specs=whole(),
        scratch_shapes=[pltpu.SemaphoreType.DMA((len(sources),))],
        cost_estimate=pl.CostEstimate(flops=0, bytes_accessed=4 * len(sources) * HALF * channels, transcendentals=0),
        compiler_params=grant(4),
        name="stack",
    )(half, *sources)


def notes_kernel(place_ref, moved_ref, slots_ref, bias_ref, notes):
    groups, lines, _ = notes.shape
    notes[...] = moved_ref[:, :lines, moved_ref.shape[2] - LANES :]
    y, lo, core, odd = place_ref[0], place_ref[1], place_ref[2], place_ref[3]
    width = slots_ref.shape[1]
    for g in range(groups):
        parts = notes[g, 0:2, :width].astype(jnp.float32)
        slots_ref[g : g + 1, :] = (parts[0:1] * 16.0 + parts[1:2]).astype(jnp.int32)

    def half(step, other, turn):
        shard = lax.rem(y + step + 4, 4) * 4 + lo * 2 + (1 - core if other else core)
        lines = notes[shard, :, : HALF // 2].astype(jnp.float32)
        one, two = [lines[2:3], lines[3:4]], [lines[4:5], lines[5:6]]
        if turn is None:
            return one + two
        pick = jnp.full(one[0].shape, odd, jnp.int32) == (1 - turn)
        return [jnp.where(pick, q, p) for p, q in zip(one, two)]

    ahead = 2 * core - 1
    early, late = half(0, False, None) + half(0, True, None), []
    for turn, group in ((0, early), (1, late)):
        for step, other in ((ahead, False), (ahead, True), (-ahead, True), (-ahead, False)):
            group += half(step, other, turn)
    for turn, other in ((0, False), (0, True), (1, False), (1, True)):
        late += half(2, other, turn)
    for k, group in enumerate((early, late)):
        for j in range(0, len(group), 4):
            at = slice(j * HALF // 2, (j + 4) * HALF // 2)
            bias_ref[k : k + 1, at] = jnp.concatenate(group[j : j + 4], axis=1)


def read_notes(place, moved):
    groups, width = moved.shape[:2]
    return pl.pallas_call(
        notes_kernel,
        out_shape=[
            jax.ShapeDtypeStruct((groups, width), jnp.int32),
            jax.ShapeDtypeStruct((2, 8 * HALF), jnp.float32),
        ],
        in_specs=[whole(pltpu.SMEM), whole()],
        out_specs=[whole(), whole()],
        scratch_shapes=[VMEM((groups, 8, LANES), jnp.bfloat16)],
        compiler_params=grant(7),
        name="notes",
    )(place, moved)


def conv_kernel(bands, *refs):
    grid_ref, left_ref, right_ref, weight_ref, vector_ref = refs[:5]
    out_ref, even, odd, both, conv = refs[-5:]
    channels = grid_ref.shape[2]
    tiles = channels // LANES
    spans = (slice(5, 8), slice(8, 24), slice(24, 27))

    def tile(t, carry):
        at = pl.ds(pl.multiple_of(t * LANES, LANES), LANES)

        def row(k):
            if 0 <= k < TH:
                parts = (left_ref[k, :, at], grid_ref[k, :, at], right_ref[k, :, at])
            else:
                edge, k = (refs[5], k + HALO) if k < 0 else (refs[6], k - TH)
                parts = (edge[k, TW : TW + HALO, at], edge[k, :TW, at], edge[k, TW + HALO :, at])
            return [part.astype(jnp.float32) for part in parts]

        base = jnp.broadcast_to(vector_ref[0:1, at], (TW, LANES))
        zero = jnp.zeros((TW, LANES), jnp.float32)
        slot, line = 0, 0
        for start, size in bands:
            pairs = size // 2
            count = pairs + HALO
            for k in range(count):
                top = start - HALO + 2 * k
                for span, e, o in zip(spans, row(top), row(top + 1)):
                    even[slot + k, span, :] = e
                    odd[slot + k, span, :] = o
                    both[slot + k, span, :] = e + o
            p, q, s = [zero] * pairs, [zero] * (pairs + 1), [zero] * pairs
            for along in range(7):
                h = [weight_ref[across, along : along + 1, at] for across in range(7)]
                mixed = [h[0]] + [h[2 * j] + h[2 * j - 1] for j in range(1, 4)]
                h, mixed = [[jnp.broadcast_to(v, (TW, LANES)) for v in group] for group in (h, mixed)]
                cols = slice(5 + along, 5 + along + TW)
                for k in range(count):
                    e, o, b = [ref[slot + k, cols, :] for ref in (even, odd, both)]
                    for j in range(4):
                        if 0 <= k - j < pairs:
                            p[k - j] = p[k - j] + e * h[2 * j]
                            s[k - j] = s[k - j] + b * mixed[j]
                    for j in range(3):
                        if 0 <= k - j <= pairs:
                            q[k - j] = q[k - j] + o * h[2 * j + 1]
            for k in range(pairs):
                conv[t, line : line + TW, :] = p[k] + q[k] + base
                conv[t, line + TW : line + 2 * TW, :] = s[k] - p[k] - q[k + 1] + base
                line += 2 * TW
            slot += count
        return carry

    lax.fori_loop(0, tiles, tile, 0)

    def norm(b, carry):
        rows = pl.ds(pl.multiple_of(b * 16, 16), 16)
        values = [conv[t, rows, :] for t in range(tiles)]
        mean = jnp.sum(sum(values), axis=-1, keepdims=True) * (1.0 / channels)
        centred = [v - mean for v in values]
        var = jnp.sum(sum(v * v for v in centred), axis=-1, keepdims=True) * (1.0 / channels)
        inverse = lax.rsqrt(var + 1e-06)
        for t in range(tiles):
            at = slice(t * LANES, (t + 1) * LANES)
            out_ref[rows, at] = (centred[t] * inverse * vector_ref[1:2, at] + vector_ref[2:3, at]).astype(
                jnp.bfloat16
            )
        return carry

    lax.fori_loop(0, out_ref.shape[0] // 16, norm, 0, unroll=2)


def conv_norm(bands, grid, left, right, weight, vectors, *edges):
    channels = grid.shape[2]
    rows = sum(size for _, size in bands)
    stage = VMEM((sum(size // 2 + HALO for _, size in bands), 32, LANES), jnp.float32)
    return pl.pallas_call(
        functools.partial(conv_kernel, bands),
        out_shape=jax.ShapeDtypeStruct((rows * TW, channels), jnp.bfloat16),
        in_specs=[whole()] * (5 + len(edges)),
        out_specs=whole(),
        scratch_shapes=[stage, stage, stage, VMEM((channels // LANES, rows * TW, LANES), jnp.float32)],
        cost_estimate=pl.CostEstimate(
            flops=100 * rows * TW * channels, bytes_accessed=8 * rows * TW * channels, transcendentals=0
        ),
        compiler_params=grant(14),
        name="conv",
    )(grid, left, right, weight, vectors, *edges)


PHI = (
    0.7978849411010742, 0.03633308410644531, -3.259496588725597e-05, -5.5306198191829026e-05,
    3.964745246776147e-06, -1.3226342332472996e-07, 1.7561730958348676e-09,
)


def gelu(pre):
    s = pre * pre
    p = PHI[-1]
    for c in PHI[-2::-1]:
        p = p * s + c
    half = 0.5 * pre
    return half + half * jnp.tanh(pre * p)


def mlp_kernel(plan, bias_at, bands, count, adds, *refs):
    rows_refs, bias_ref = refs[:bands], refs[bands]
    pieces = refs[bands + 1 : bands + 1 + count]
    acc_ref = refs[bands + 1 + count] if adds else None
    out_ref, rows, w_in, w_out, hid, sems, row_sems = refs[bands + 1 + count + adds :]
    blocks = w_in.shape[0] // UNITS
    columns = w_out.shape[1] // UNITS
    ins, outs, at = [], [], 0
    for k, (a, row_a, b, row_b, size) in enumerate(plan):
        ins.append(pltpu.make_async_copy(pieces[a].at[pl.ds(row_a, size)], w_in.at[pl.ds(at, size)], sems.at[k, 0]))
        outs.append(pltpu.make_async_copy(pieces[b].at[pl.ds(row_b, size)], w_out.at[pl.ds(at, size)], sems.at[k, 1]))
        at += size
    moves = []
    for ref, group in zip(rows_refs, (MIDDLE, EDGES)):
        line = 0
        for start, size in group:
            source, target = ref.at[pl.ds(line * TW, size * TW)], rows.at[pl.ds(start * TW, size * TW)]
            moves.append(pltpu.make_async_copy(source, target, row_sems.at[len(moves)]))
            line += size
    early = next(k for k in range(len(plan) + 1) if sum(p[4] for p in plan[:k]) >= blocks // 2 * UNITS)
    for copy in moves + ins + outs:
        copy.start()
    for copy in moves + ins[:early]:
        copy.wait()

    def first(h):
        return lax.dot_general(
            rows[...], w_in[h * UNITS : (h + 1) * UNITS, :], (((1,), (1,)), ((), ())),
            preferred_element_type=jnp.float32,
        )

    def middle(h, pre):
        at = slice(h * UNITS, (h + 1) * UNITS)
        hid[:, at] = gelu(pre + bias_ref[bias_at[0] : bias_at[0] + 1, bias_at[1] + h * UNITS : bias_at[1] + (h + 1) * UNITS]).astype(jnp.bfloat16)

    waiting = None
    for h in range(blocks):
        if h == blocks // 2:
            for copy in ins[early:] + outs:
                copy.wait()
        pre = first(h)
        if waiting is not None:
            middle(*waiting)
        waiting = (h, pre)
    middle(*waiting)
    for n in range(columns):
        at = slice(n * UNITS, (n + 1) * UNITS)
        total = jnp.dot(hid[...], w_out[:, at], preferred_element_type=jnp.float32)
        if adds:
            total = total + acc_ref[:, at]
        out_ref[:, at] = total.astype(out_ref.dtype)


def mlp(rows, bias, bias_at, pieces, plan, acc=None, out_dtype=jnp.float32):
    m, channels = sum(part.shape[0] for part in rows), rows[0].shape[1]
    hidden = sum(p[4] for p in plan)
    adds = acc is not None
    return pl.pallas_call(
        functools.partial(mlp_kernel, plan, bias_at, len(rows), len(pieces), int(adds)),
        out_shape=jax.ShapeDtypeStruct((m, channels), out_dtype),
        in_specs=[whole(pl.ANY)] * len(rows) + [whole()] + [whole(pl.ANY)] * len(pieces) + [whole()] * adds,
        out_specs=whole(),
        scratch_shapes=[
            VMEM((m, channels), jnp.bfloat16),
            VMEM((hidden, channels), jnp.bfloat16),
            VMEM((hidden, channels), jnp.bfloat16),
            VMEM((m, hidden), jnp.bfloat16),
            pltpu.SemaphoreType.DMA((len(plan), 2)),
            pltpu.SemaphoreType.DMA((len(MIDDLE + EDGES),)),
        ],
        cost_estimate=pl.CostEstimate(
            flops=4 * m * hidden * channels, bytes_accessed=4 * hidden * channels, transcendentals=m * hidden
        ),
        compiler_params=grant(28),
        name="mlp",
    )(*rows, bias, *pieces, *([acc] if adds else []))


def local(
    patches,
    dest,
    background,
    conv_weight,
    conv_bias,
    norm_gain,
    norm_bias,
    w_in,
    b_in,
    w_out,
    b_out,
    layer_scale,
):
    cells = TH * TW
    channels = patches.shape[1]
    row, col = lax.axis_index("row"), lax.axis_index("col")
    my_y, my_lo, my_core, my_h = col // 4, (col // 2) % 2, col % 2, (row // 2) % 2

    slots = dest.reshape(16, 1, 48)
    parts = jnp.concatenate([slots >> 4, slots & 15], axis=1).astype(jnp.bfloat16)
    ours = jnp.broadcast_to(b_in.reshape(1, 4, HALF // 2), (16, 4, HALF // 2))
    head = jnp.concatenate(
        [jnp.pad(parts, ((0, 0), (0, 0), (0, 80))), jnp.pad(ours, ((0, 0), (0, 2), (0, 32)))], axis=1
    )
    moved = lax.all_to_all(join(patches, head), "col", split_axis=0, concat_axis=0, tiled=True)

    half = my_h.astype(jnp.int32).reshape(1)
    near_a = send(stack(half, w_in, w_out), along_y)
    w_in_p, w_out_p = send(w_in, to_partner), send(w_out, to_partner)
    near_b = send(stack(half, w_in_p, w_out_p), along_y)
    near_a_z = send(near_a, along_z)
    far = send(near_a, along_y)
    near_a_p = send(near_a, to_partner)
    near_b_z = send(near_b, along_z)
    near_b_p = send(near_b, to_partner)
    far_z = send(far, along_z)
    far_p = send(far, to_partner)
    near_a_zp = send(near_a_z, to_partner)
    near_b_zp = send(near_b_z, to_partner)
    far_zp = send(far_z, to_partner)

    early = (w_in, w_out, w_in_p, w_out_p, near_a, near_b, near_a_p, near_b_p)
    early_plan = ((0, 0, 1, 0, SHARD), (2, 0, 3, 0, SHARD)) + tuple((a, 0, a, HALF, HALF) for a in range(4, 8))
    mid = (near_a_z, near_b_z, near_a_zp, near_b_zp)
    late = (far, far_p, far_z, far_zp)

    def halves(count):
        return tuple((a, 0, a, HALF, HALF) for a in range(count))

    place = jnp.stack([my_y, my_lo, my_core, my_h]).astype(jnp.int32)
    vectors = jnp.stack([conv_bias, norm_gain, norm_bias])
    moved, vectors, place = lax.optimization_barrier((moved, vectors, place))
    where, bias = read_notes(place, moved.reshape(16, 48, -1))
    where = where.reshape(-1)
    onehot = where[None, :] == jnp.arange(cells, dtype=jnp.int32)[:, None]
    placed = jnp.dot(
        onehot.astype(jnp.bfloat16), moved[:, :channels], preferred_element_type=jnp.float32
    )
    present = jnp.any(onehot, axis=1)
    grid = jnp.where(present[:, None], placed, background.astype(jnp.float32)[None, :]).astype(
        jnp.bfloat16
    )
    block = grid.reshape(TH, TW, channels)
    left = shift(block[:, TW - HALO :], "col", 1)
    right = shift(block[:, :HALO], "col", -1)
    top, bottom = [
        shift(jnp.concatenate([part[cut] for part in (block, left, right)], axis=1), "row", step)
        for cut, step in ((slice(TH - HALO, TH), 1), (slice(0, HALO), -1))
    ]
    flat_a = conv_norm(MIDDLE, block, left, right, conv_weight, vectors)
    flat_b = conv_norm(EDGES, block, left, right, conv_weight, vectors, top, bottom)

    flat = (flat_a, flat_b)
    other = (send(flat_a, along_x), send(flat_b, along_x))
    mine = mlp(flat, bias, (0, 0), early, early_plan)
    theirs = mlp(other, bias, (0, 0), early, early_plan)
    theirs = mlp(other, bias, (1, 0), mid, halves(4), acc=theirs)
    theirs = mlp(other, bias, (1, 4 * HALF), late, halves(4), acc=theirs, out_dtype=jnp.bfloat16)
    returned = send(theirs, back_x)
    mine = mlp(flat, bias, (1, 0), mid + late, halves(8), acc=mine)
    mixed = mine + returned.astype(jnp.float32)
    result = grid.astype(jnp.float32) + layer_scale * (mixed + b_out)
    return result.astype(jnp.bfloat16).reshape(TH, TW, channels)


def solution(mesh):
    placed = (
        P(("row", "col"), None),
        P(("row", "col")),
        P(),
        P(),
        P(),
        P(),
        P(),
        P("col", None),
        P("col"),
        P("col", None),
        P(),
        P(),
    )

    def step(*args):
        return local(*args)

    step = jax.shard_map(
        step, mesh=mesh, in_specs=placed, out_specs=P("row", "col", None), check_vma=False
    )
    return step
```

```python
import functools

import jax
import jax.numpy as jnp
from jax import lax
from jax.experimental import pallas as pl
from jax.experimental.pallas import tpu as pltpu
from jax.sharding import PartitionSpec as P


TH = 32
TW = 16
SHARD = 384
HALF = SHARD // 2
LANES = 128
HALO = 3
MIDDLE = ((8, 16),)
EDGES = ((0, 8), (24, 8))
UNITS = 256

VMEM = pltpu.VMEM


def device_index(x, y, z, core):
    x, y, z = x % 4, y % 4, z % 4
    return (z * 2 + x // 2) * 16 + y * 4 + (x % 2) * 2 + core


def routes(move):
    return [
        (device_index(x, y, z, core), device_index(*move(x, y, z, core)))
        for x in range(4)
        for y in range(4)
        for z in range(4)
        for core in range(2)
    ]


def send(value, move):
    return lax.ppermute(value, ("row", "col"), routes(move))


def to_partner(x, y, z, core):
    return x, y, z, 1 - core


def along_y(x, y, z, core):
    return x, y + 1 - 2 * core, z, core


def along_z(x, y, z, core):
    return x, y, z + 1 - 2 * core, core


def along_x(x, y, z, core):
    return x + 1 - 2 * core, y, z, core


def back_x(x, y, z, core):
    return x - 1 + 2 * core, y, z, core


def shift(value, axis, step):
    last = lax.axis_size(axis) - 1
    pairs = [(i, i + 1) if step > 0 else (i + 1, i) for i in range(last)]
    return lax.ppermute(value, axis, pairs)


def whole(space=VMEM):
    return pl.BlockSpec(memory_space=space)


def grant(mib):
    return pltpu.CompilerParams(vmem_limit_bytes=mib * 1024 * 1024)


def join_kernel(patches_ref, head_ref, out_ref, rows, sems):
    channels = patches_ref.shape[1]
    parts = [pl.ds(k * rows.shape[0] // 4, rows.shape[0] // 4) for k in range(4)]
    ins = [
        pltpu.make_async_copy(patches_ref.at[part], rows.at[part, pl.ds(0, channels)], sems.at[0, k])
        for k, part in enumerate(parts)
    ]
    outs = [pltpu.make_async_copy(rows.at[part], out_ref.at[part], sems.at[1, k]) for k, part in enumerate(parts)]
    for copy in ins:
        copy.start()
    groups, lines, _ = head_ref.shape
    size = rows.shape[0] // groups
    rows[:, channels:] = jnp.zeros((rows.shape[0], LANES), rows.dtype)
    for g in range(groups):
        rows[g * size : g * size + lines, channels:] = head_ref[g]
    for arrived, leaves in zip(ins, outs):
        arrived.wait()
        leaves.start()
    for copy in outs:
        copy.wait()


def join(patches, head):
    rows, channels = patches.shape
    return pl.pallas_call(
        join_kernel,
        out_shape=jax.ShapeDtypeStruct((rows, channels + LANES), patches.dtype),
        in_specs=[whole(pl.ANY), whole()],
        out_specs=whole(pl.ANY),
        scratch_shapes=[VMEM((rows, channels + LANES), patches.dtype), pltpu.SemaphoreType.DMA((2, 4))],
        cost_estimate=pl.CostEstimate(flops=0, bytes_accessed=4 * rows * channels, transcendentals=0),
        name="join",
    )(patches, head)


def stack_kernel(half_ref, *refs):
    *sources, out_ref, sems = refs
    start = pl.multiple_of(half_ref[0] * HALF, HALF)
    copies = [
        pltpu.make_async_copy(source.at[pl.ds(start, HALF)], out_ref.at[pl.ds(k * HALF, HALF)], sems.at[k])
        for k, source in enumerate(sources)
    ]
    for copy in copies:
        copy.start()
    for copy in copies:
        copy.wait()


def stack(half, *sources):
    channels = sources[0].shape[1]
    return pl.pallas_call(
        stack_kernel,
        out_shape=jax.ShapeDtypeStruct((len(sources) * HALF, channels), jnp.bfloat16),
        in_specs=[whole(pltpu.SMEM)] + [whole(pl.ANY)] * len(sources),
        out_specs=whole(),
        scratch_shapes=[pltpu.SemaphoreType.DMA((len(sources),))],
        cost_estimate=pl.CostEstimate(flops=0, bytes_accessed=4 * len(sources) * HALF * channels, transcendentals=0),
        compiler_params=grant(4),
        name="stack",
    )(half, *sources)


def notes_kernel(place_ref, moved_ref, slots_ref, bias_ref, notes):
    groups, lines, _ = notes.shape
    notes[...] = moved_ref[:, :lines, moved_ref.shape[2] - LANES :]
    y, lo, core, odd = place_ref[0], place_ref[1], place_ref[2], place_ref[3]
    width = slots_ref.shape[1]
    for g in range(groups):
        parts = notes[g, 0:2, :width].astype(jnp.float32)
        slots_ref[g : g + 1, :] = (parts[0:1] * 16.0 + parts[1:2]).astype(jnp.int32)

    def half(step, other, turn):
        shard = lax.rem(y + step + 4, 4) * 4 + lo * 2 + (1 - core if other else core)
        lines = notes[shard, :, : HALF // 2].astype(jnp.float32)
        one, two = [lines[2:3], lines[3:4]], [lines[4:5], lines[5:6]]
        if turn is None:
            return one + two
        pick = jnp.full(one[0].shape, odd, jnp.int32) == (1 - turn)
        return [jnp.where(pick, q, p) for p, q in zip(one, two)]

    ahead = 2 * core - 1
    early, late = half(0, False, None) + half(0, True, None), []
    for turn, group in ((0, early), (1, late)):
        for step, other in ((ahead, False), (ahead, True), (-ahead, True), (-ahead, False)):
            group += half(step, other, turn)
    for turn, other in ((0, False), (0, True), (1, False), (1, True)):
        late += half(2, other, turn)
    for k, group in enumerate((early, late)):
        for j in range(0, len(group), 4):
            at = slice(j * HALF // 2, (j + 4) * HALF // 2)
            bias_ref[k : k + 1, at] = jnp.concatenate(group[j : j + 4], axis=1)


def read_notes(place, moved):
    groups, width = moved.shape[:2]
    return pl.pallas_call(
        notes_kernel,
        out_shape=[
            jax.ShapeDtypeStruct((groups, width), jnp.int32),
            jax.ShapeDtypeStruct((2, 8 * HALF), jnp.float32),
        ],
        in_specs=[whole(pltpu.SMEM), whole()],
        out_specs=[whole(), whole()],
        scratch_shapes=[VMEM((groups, 8, LANES), jnp.bfloat16)],
        compiler_params=grant(7),
        name="notes",
    )(place, moved)


def conv_kernel(bands, *refs):
    grid_ref, left_ref, right_ref, weight_ref, vector_ref = refs[:5]
    out_ref, even, odd, both, conv = refs[-5:]
    channels = grid_ref.shape[2]
    tiles = channels // LANES
    spans = (slice(5, 8), slice(8, 24), slice(24, 27))

    def tile(t, carry):
        at = pl.ds(pl.multiple_of(t * LANES, LANES), LANES)

        def row(k):
            if 0 <= k < TH:
                parts = (left_ref[k, :, at], grid_ref[k, :, at], right_ref[k, :, at])
            else:
                edge, k = (refs[5], k + HALO) if k < 0 else (refs[6], k - TH)
                parts = (edge[k, TW : TW + HALO, at], edge[k, :TW, at], edge[k, TW + HALO :, at])
            return [part.astype(jnp.float32) for part in parts]

        base = jnp.broadcast_to(vector_ref[0:1, at], (TW, LANES))
        zero = jnp.zeros((TW, LANES), jnp.float32)
        slot, line = 0, 0
        for start, size in bands:
            pairs = size // 2
            count = pairs + HALO
            for k in range(count):
                top = start - HALO + 2 * k
                for span, e, o in zip(spans, row(top), row(top + 1)):
                    even[slot + k, span, :] = e
                    odd[slot + k, span, :] = o
                    both[slot + k, span, :] = e + o
            p, q, s = [zero] * pairs, [zero] * (pairs + 1), [zero] * pairs
            for along in range(7):
                h = [weight_ref[across, along : along + 1, at] for across in range(7)]
                mixed = [h[0]] + [h[2 * j] + h[2 * j - 1] for j in range(1, 4)]
                h, mixed = [[jnp.broadcast_to(v, (TW, LANES)) for v in group] for group in (h, mixed)]
                cols = slice(5 + along, 5 + along + TW)
                for k in range(count):
                    e, o, b = [ref[slot + k, cols, :] for ref in (even, odd, both)]
                    for j in range(4):
                        if 0 <= k - j < pairs:
                            p[k - j] = p[k - j] + e * h[2 * j]
                            s[k - j] = s[k - j] + b * mixed[j]
                    for j in range(3):
                        if 0 <= k - j <= pairs:
                            q[k - j] = q[k - j] + o * h[2 * j + 1]
            for k in range(pairs):
                conv[t, line : line + TW, :] = p[k] + q[k] + base
                conv[t, line + TW : line + 2 * TW, :] = s[k] - p[k] - q[k + 1] + base
                line += 2 * TW
            slot += count
        return carry

    lax.fori_loop(0, tiles, tile, 0)

    def norm(b, carry):
        rows = pl.ds(pl.multiple_of(b * 16, 16), 16)
        values = [conv[t, rows, :] for t in range(tiles)]
        mean = jnp.sum(sum(values), axis=-1, keepdims=True) * (1.0 / channels)
        centred = [v - mean for v in values]
        var = jnp.sum(sum(v * v for v in centred), axis=-1, keepdims=True) * (1.0 / channels)
        inverse = lax.rsqrt(var + 1e-06)
        for t in range(tiles):
            at = slice(t * LANES, (t + 1) * LANES)
            out_ref[rows, at] = (centred[t] * inverse * vector_ref[1:2, at] + vector_ref[2:3, at]).astype(
                jnp.bfloat16
            )
        return carry

    lax.fori_loop(0, out_ref.shape[0] // 16, norm, 0, unroll=2)


def conv_norm(bands, grid, left, right, weight, vectors, *edges):
    channels = grid.shape[2]
    rows = sum(size for _, size in bands)
    stage = VMEM((sum(size // 2 + HALO for _, size in bands), 32, LANES), jnp.float32)
    return pl.pallas_call(
        functools.partial(conv_kernel, bands),
        out_shape=jax.ShapeDtypeStruct((rows * TW, channels), jnp.bfloat16),
        in_specs=[whole()] * (5 + len(edges)),
        out_specs=whole(),
        scratch_shapes=[stage, stage, stage, VMEM((channels // LANES, rows * TW, LANES), jnp.float32)],
        cost_estimate=pl.CostEstimate(
            flops=100 * rows * TW * channels, bytes_accessed=8 * rows * TW * channels, transcendentals=0
        ),
        compiler_params=grant(14),
        name="conv",
    )(grid, left, right, weight, vectors, *edges)


PHI = (
    0.7978849411010742, 0.03633308410644531, -3.259496588725597e-05, -5.5306198191829026e-05,
    3.964745246776147e-06, -1.3226342332472996e-07, 1.7561730958348676e-09,
)


def gelu(pre):
    s = pre * pre
    p = PHI[-1]
    for c in PHI[-2::-1]:
        p = p * s + c
    half = 0.5 * pre
    return half + half * jnp.tanh(pre * p)


def mlp_kernel(plan, bias_at, bands, count, adds, *refs):
    rows_refs, bias_ref = refs[:bands], refs[bands]
    pieces = refs[bands + 1 : bands + 1 + count]
    acc_ref = refs[bands + 1 + count] if adds else None
    out_ref, rows, w_in, w_out, hid, sems, row_sems = refs[bands + 1 + count + adds :]
    blocks = w_in.shape[0] // UNITS
    columns = w_out.shape[1] // UNITS
    ins, outs, at = [], [], 0
    for k, (a, row_a, b, row_b, size) in enumerate(plan):
        ins.append(pltpu.make_async_copy(pieces[a].at[pl.ds(row_a, size)], w_in.at[pl.ds(at, size)], sems.at[k, 0]))
        outs.append(pltpu.make_async_copy(pieces[b].at[pl.ds(row_b, size)], w_out.at[pl.ds(at, size)], sems.at[k, 1]))
        at += size
    moves = []
    for ref, group in zip(rows_refs, (MIDDLE, EDGES)):
        line = 0
        for start, size in group:
            source, target = ref.at[pl.ds(line * TW, size * TW)], rows.at[pl.ds(start * TW, size * TW)]
            moves.append(pltpu.make_async_copy(source, target, row_sems.at[len(moves)]))
            line += size
    for copy in moves + ins + outs:
        copy.start()
    for copy in moves + ins + outs:
        copy.wait()

    half_rows = rows.shape[0] // 2

    def cut(r):
        return slice(r * half_rows, (r + 1) * half_rows)

    waiting, sent = None, 0
    todo = [(r, n) for r in range(2) for n in range(columns)]

    def finish(r, n):
        at = slice(n * UNITS, (n + 1) * UNITS)
        total = jnp.dot(hid[cut(r), :], w_out[:, at], preferred_element_type=jnp.float32)
        if adds:
            total = total + acc_ref[cut(r), at]
        out_ref[cut(r), at] = total.astype(out_ref.dtype)

    def activate(r, h, pre):
        at = slice(h * UNITS, (h + 1) * UNITS)
        hid[cut(r), at] = gelu(pre + bias_ref[bias_at[0] : bias_at[0] + 1, bias_at[1] + h * UNITS : bias_at[1] + (h + 1) * UNITS]).astype(jnp.bfloat16)

    for k in range(2 * blocks):
        r, h = divmod(k, blocks)
        pre = lax.dot_general(
            rows[cut(r), :], w_in[h * UNITS : (h + 1) * UNITS, :], (((1,), (1,)), ((), ())),
            preferred_element_type=jnp.float32,
        )
        if waiting is not None:
            activate(*waiting)
        waiting = (r, h, pre)
        if k > blocks:
            finish(*todo[sent])
            sent += 1
    activate(*waiting)
    for item in todo[sent:]:
        finish(*item)


def mlp(rows, bias, bias_at, pieces, plan, acc=None, out_dtype=jnp.float32):
    m, channels = sum(part.shape[0] for part in rows), rows[0].shape[1]
    hidden = sum(p[4] for p in plan)
    adds = acc is not None
    return pl.pallas_call(
        functools.partial(mlp_kernel, plan, bias_at, len(rows), len(pieces), int(adds)),
        out_shape=jax.ShapeDtypeStruct((m, channels), out_dtype),
        in_specs=[whole(pl.ANY)] * len(rows) + [whole()] + [whole(pl.ANY)] * len(pieces) + [whole()] * adds,
        out_specs=whole(),
        scratch_shapes=[
            VMEM((m, channels), jnp.bfloat16),
            VMEM((hidden, channels), jnp.bfloat16),
            VMEM((hidden, channels), jnp.bfloat16),
            VMEM((m, hidden), jnp.bfloat16),
            pltpu.SemaphoreType.DMA((len(plan), 2)),
            pltpu.SemaphoreType.DMA((len(MIDDLE + EDGES),)),
        ],
        cost_estimate=pl.CostEstimate(
            flops=4 * m * hidden * channels, bytes_accessed=4 * hidden * channels, transcendentals=m * hidden
        ),
        compiler_params=grant(28),
        name="mlp",
    )(*rows, bias, *pieces, *([acc] if adds else []))


def local(
    patches,
    dest,
    background,
    conv_weight,
    conv_bias,
    norm_gain,
    norm_bias,
    w_in,
    b_in,
    w_out,
    b_out,
    layer_scale,
):
    cells = TH * TW
    channels = patches.shape[1]
    row, col = lax.axis_index("row"), lax.axis_index("col")
    my_y, my_lo, my_core, my_h = col // 4, (col // 2) % 2, col % 2, (row // 2) % 2

    slots = dest.reshape(16, 1, 48)
    parts = jnp.concatenate([slots >> 4, slots & 15], axis=1).astype(jnp.bfloat16)
    ours = jnp.broadcast_to(b_in.reshape(1, 4, HALF // 2), (16, 4, HALF // 2))
    head = jnp.concatenate(
        [jnp.pad(parts, ((0, 0), (0, 0), (0, 80))), jnp.pad(ours, ((0, 0), (0, 2), (0, 32)))], axis=1
    )
    moved = lax.all_to_all(join(patches, head), "col", split_axis=0, concat_axis=0, tiled=True)

    half = my_h.astype(jnp.int32).reshape(1)
    near_a = send(stack(half, w_in, w_out), along_y)
    w_in_p, w_out_p = send(w_in, to_partner), send(w_out, to_partner)
    near_b = send(stack(half, w_in_p, w_out_p), along_y)
    near_a_z = send(near_a, along_z)
    far = send(near_a, along_y)
    near_a_p = send(near_a, to_partner)
    near_b_z = send(near_b, along_z)
    near_b_p = send(near_b, to_partner)
    far_z = send(near_a_z, along_y)
    far_p = send(far, to_partner)
    near_a_zp = send(near_a_z, to_partner)
    near_b_zp = send(near_b_z, to_partner)
    far_zp = send(far_z, to_partner)

    early = (w_in, w_out, w_in_p, w_out_p, near_a, near_b, near_a_p, near_b_p)
    early_plan = ((0, 0, 1, 0, SHARD), (2, 0, 3, 0, SHARD)) + tuple((a, 0, a, HALF, HALF) for a in range(4, 8))
    mid = (near_a_z, near_b_z, near_a_zp, near_b_zp)
    late = (far, far_p, far_z, far_zp)

    def halves(count):
        return tuple((a, 0, a, HALF, HALF) for a in range(count))

    place = jnp.stack([my_y, my_lo, my_core, my_h]).astype(jnp.int32)
    vectors = jnp.stack([conv_bias, norm_gain, norm_bias])
    moved, vectors, place = lax.optimization_barrier((moved, vectors, place))
    where, bias = read_notes(place, moved.reshape(16, 48, -1))
    where = where.reshape(-1)
    onehot = where[None, :] == jnp.arange(cells, dtype=jnp.int32)[:, None]
    placed = jnp.dot(
        onehot.astype(jnp.bfloat16), moved[:, :channels], preferred_element_type=jnp.float32
    )
    present = jnp.any(onehot, axis=1)
    grid = jnp.where(present[:, None], placed, background.astype(jnp.float32)[None, :]).astype(
        jnp.bfloat16
    )
    block = grid.reshape(TH, TW, channels)
    left = shift(block[:, TW - HALO :], "col", 1)
    right = shift(block[:, :HALO], "col", -1)
    top, bottom = [
        shift(jnp.concatenate([part[cut] for part in (block, left, right)], axis=1), "row", step)
        for cut, step in ((slice(TH - HALO, TH), 1), (slice(0, HALO), -1))
    ]
    flat_a = conv_norm(MIDDLE, block, left, right, conv_weight, vectors)
    flat_b = conv_norm(EDGES, block, left, right, conv_weight, vectors, top, bottom)

    flat = (flat_a, flat_b)
    other = (send(flat_a, along_x), send(flat_b, along_x))
    mine = mlp(flat, bias, (0, 0), early, early_plan)
    theirs = mlp(other, bias, (0, 0), early, early_plan)
    theirs = mlp(other, bias, (1, 0), mid, halves(4), acc=theirs)
    theirs = mlp(other, bias, (1, 4 * HALF), late, halves(4), acc=theirs, out_dtype=jnp.bfloat16)
    returned = send(theirs, back_x)
    mine = mlp(flat, bias, (1, 0), mid + late, halves(8), acc=mine)
    mixed = mine + returned.astype(jnp.float32)
    result = grid.astype(jnp.float32) + layer_scale * (mixed + b_out)
    return result.astype(jnp.bfloat16).reshape(TH, TW, channels)


def solution(mesh):
    placed = (
        P(("row", "col"), None),
        P(("row", "col")),
        P(),
        P(),
        P(),
        P(),
        P(),
        P("col", None),
        P("col"),
        P("col", None),
        P(),
        P(),
    )

    def step(*args):
        return local(*args)

    step = jax.shard_map(
        step, mesh=mesh, in_specs=placed, out_specs=P("row", "col", None), check_vma=False
    )
    return step
```
